128 devices in a mesh: dom: 32 (over z, x, core), dir: 4 (over y).
Axes of the slice: x: 4, y: 4, z: 4, core: 2. Of those that a mesh axis runs over, the one named last changes fastest.
Arguments:
- x_edges: bfloat16 [262144, 128], P(('dom', 'dir')), may hold values from -6 to 6
- send_list: int32 [16384, 32], P(('dom', 'dir')), may hold values from 0 to 2048, as said below
- connectivity: int32 [6, 131072], P(None, ('dom', 'dir')), may hold values from 0 to 6143, as said below
- elem_mats: float32 [36, 131072], P(None, ('dom', 'dir'))
- elem_live: int32 [128], P(('dom', 'dir')), may hold values from 512 to 1024, as said below
- currents: bfloat16 [4096, 128, 128], P(('dom', 'dir')), may hold values from -0.1796875 to 0.1796875
- positions: bfloat16 [4096, 3, 128], P(('dom', 'dir')), may hold values from -1 to 1
- block_live: int32 [4096], P(('dom', 'dir')), may hold values from 32 to 128
- block_owner: int32 [4096], P(('dom', 'dir')), may hold values from 0 to 31, as said below
- block_leaf: int32 [4096], P(('dom', 'dir')), may hold values from 0 to 15
- cone_waves: float32 [3, 16], P(None, 'dir'), may hold values from -6 to 6
Outputs:
- interior_out: float32 [262144, 128], P(('dom', 'dir'))
- expansions: float32 [64, 16, 2, 64, 128], P('dom', 'dir')
The draws below stay inside these ranges and needn't reach their ends.
Inputs may be any that keep to these rules, and one draw needn't show every extreme that they name: `send_list`: in row a * 128 + b the used entries come first and name owned edges of a; the rest are 2048. A partition reads nothing of itself; some pair uses all 32 entries. `connectivity`: entries below 2048 are owned edges; 2048 + p * 32 + s names the s-th edge that partition p lists for this partition, and only used entries are named. `elem_live`: elements at positions from this count on are padding; some partition has all 1024. `block_owner`: among the 32 blocks of one partition at most 3 name one leaf owner; some leaf owner is named by exactly 3 blocks of every partition.
All inputs are finite; a program needn't handle non-finite values.
Results may differ from the reference program's by a relative error of at most 0.0056.
Values may be sent and summed in bfloat16 or wider, within the bound.
No kernel may reach another device: no remote copies, remote signals or barrier semaphores. Data moves between devices by JAX's collectives and lax.ppermute only.
A program may use at most 128 MiB of HBM per device.

```python
import jax
import jax.numpy as jnp
from jax import lax

E_OWN = 2048
EL_DEV = 1024
HS = 32
NRHS = 128
BS = 128
BLK_DEV = 32
LEAVES_DEV = 16
NODES = 4
PARTITIONS = 128
OWNERS = 32
EDGES = 262144
ELEMENTS = 131072
BLOCKS = 4096
CAP = 3
LEAVES = 512
CONES = 16


def halo_counts(key):
    base_key = jax.random.fold_in(key, 7001)
    first_key, second_key, third_key, extra_key = jax.random.split(base_key, 4)
    counts = jax.random.randint(first_key, (PARTITIONS, PARTITIONS), HS // 2, HS + 1)
    rows_now = jnp.arange(PARTITIONS)[:, None]
    cols_now = jnp.arange(PARTITIONS)[None, :]
    distance = (cols_now - rows_now) % PARTITIONS
    nearby = (distance >= 1) & (distance <= 8) | (distance >= PARTITIONS - 8)
    further = jax.random.randint(extra_key, (PARTITIONS, PARTITIONS), 0, PARTITIONS) < 4
    linked = (nearby | further) & (distance != 0)
    counts = jnp.where(linked, counts, 0)
    sender = jax.random.randint(second_key, (), 0, PARTITIONS)
    stride = jax.random.randint(third_key, (), 1, PARTITIONS)
    return counts.at[sender, (sender + stride) % PARTITIONS].set(HS)


def draw_send_list(key, part):
    counts = halo_counts(key)
    entries = jax.random.randint(jax.random.fold_in(key, 7002), (PARTITIONS * PARTITIONS, HS), 0, E_OWN)
    used_slots = jnp.arange(HS)[None, :] < counts.reshape(-1)[:, None]
    return jnp.where(used_slots, entries, E_OWN).astype(jnp.int32)


def draw_connectivity(key, part):
    counts = halo_counts(key)
    incoming = counts.T
    running = jnp.cumsum(incoming, axis=1)
    totals = running[:, -1]
    keys_all = jax.random.split(jax.random.fold_in(key, 7003), 3)
    width_all = 6 * EL_DEV
    picks = jax.random.randint(keys_all[0], (PARTITIONS, width_all), 0, 1048576) % jnp.maximum(totals, 1)[:, None]
    sender = jax.vmap(lambda row_sums, wanted: jnp.searchsorted(row_sums, wanted, side='right'))(running, picks)
    sender = jnp.minimum(sender.astype(jnp.int32), PARTITIONS - 1)
    before = jnp.take_along_axis(running, sender, axis=1) - jnp.take_along_axis(incoming, sender, axis=1)
    halo_index = E_OWN + sender * HS + (picks - before)
    local_index = jax.random.randint(keys_all[1], (PARTITIONS, width_all), 0, E_OWN)
    choose_halo = (jax.random.randint(keys_all[2], (PARTITIONS, width_all), 0, 4) == 0) & (totals[:, None] > 0)
    merged = jnp.where(choose_halo, halo_index, local_index)
    return merged.reshape(PARTITIONS, 6, EL_DEV).transpose(1, 0, 2).reshape(6, PARTITIONS * EL_DEV).astype(jnp.int32)


def draw_elem_mats(key, part):
    first_key, second_key = jax.random.split(jax.random.fold_in(key, 7004), 2)
    random_part = jax.random.uniform(first_key, (6, 6, ELEMENTS), jnp.float32, -0.35, 0.35)
    symmetric = 0.5 * (random_part + random_part.transpose(1, 0, 2))
    identity = jnp.eye(6, dtype=jnp.float32)[:, :, None]
    offdiag = symmetric * (1.0 - identity)
    lifted = jnp.sum(jnp.abs(offdiag), axis=1) + jax.random.uniform(second_key, (6, ELEMENTS), jnp.float32, 0.5, 1.5)
    matrix = offdiag + identity * lifted[:, None, :]
    return (0.3 * matrix).reshape(36, ELEMENTS)


def draw_elem_live(key, part):
    first_key, second_key = jax.random.split(jax.random.fold_in(key, 7005))
    counts = jax.random.randint(first_key, (PARTITIONS,), EL_DEV // 2, EL_DEV + 1)
    fullest = jax.random.randint(second_key, (), 0, PARTITIONS)
    return counts.at[fullest].set(EL_DEV).astype(jnp.int32)


def draw_block_owner(key, part):
    base_key = jax.random.fold_in(key, 7006)
    hot_key, device_key = jax.random.split(base_key)
    hottest = jax.random.randint(hot_key, (), 0, OWNERS)
    others = BLK_DEV - CAP

    def one_device(device):
        spread_key, order_key = jax.random.split(jax.random.fold_in(device_key, device))
        places = jax.random.permutation(spread_key, (OWNERS - 1) * CAP)[:others] // CAP
        places = jnp.where(places >= hottest, places + 1, places)
        owners_now = jnp.concatenate([jnp.full((CAP,), hottest, jnp.int32), places.astype(jnp.int32)])
        return owners_now[jax.random.permutation(order_key, BLK_DEV)]
    return jax.vmap(one_device)(jnp.arange(PARTITIONS)).reshape(-1).astype(jnp.int32)


def draw_positions(key, part):
    first_key = jax.random.fold_in(jax.random.fold_in(key, 7007), 0)
    values = jax.random.uniform(first_key, (BLOCKS, 3, BS), jnp.float32, -1.0, 1.0)
    return values.astype(jnp.bfloat16)


def draw_cone_waves(key, part):
    first_key, second_key = jax.random.split(jax.random.fold_in(key, 7008))
    magnitude = jax.random.uniform(first_key, (3, CONES), jnp.float32, 5.0, 6.0)
    signs = jnp.where(jax.random.uniform(second_key, (3, CONES), jnp.float32) < 0.5, -1.0, 1.0)
    return (signs * magnitude).astype(jnp.float32)


def touch_ends(values, key, smallest, top_value):
    longest = values.shape.index(max(values.shape))
    spots = []
    for shift in (0, 1):
        where = [jax.random.randint(jax.random.fold_in(key, axis), (), 0, length) for axis, length in enumerate(values.shape)]
        where[longest] = (where[longest] + shift) % values.shape[longest]
        spots.append(tuple(where))
    return values.at[spots[0]].set(smallest).at[spots[1]].set(top_value)


def steps_of(rng, extent, cuts, smallest, high):
    def one(position, blocks):
        steps = jax.random.uniform(jax.random.fold_in(jax.random.fold_in(rng, 6), position), (blocks,), jnp.float32, smallest / len(cuts), high / len(cuts))
        return jnp.repeat(jnp.exp(steps), extent[position] // blocks).reshape((-1,) + (1,) * (len(extent) - position - 1))

    level = one(*cuts[0])
    for cut in cuts[1:]:
        level = level * one(*cut)
    return level


def gaussian(stream_key, shape, width, bound, shards=(), held_as=jnp.bfloat16):
    level = steps_of(stream_key, shape, shards, -0.22, 0.18) if shards else 1.0
    array = jax.random.normal(stream_key, shape, jnp.float32) * width * level
    return jnp.minimum(jnp.maximum(array, -bound), bound).astype(held_as)


def setup_inputs(seed: int = 0) -> dict:
    seeds = jax.random.split(jax.random.key(seed), 12)
    x_edges = gaussian(seeds[0], (EDGES, NRHS), 1.0, 6.0, ((0, 128),))
    send_list = draw_send_list(jax.random.fold_in(seeds[11], 71), 0)
    connectivity = draw_connectivity(jax.random.fold_in(seeds[11], 71), 0)
    elem_mats = draw_elem_mats(jax.random.fold_in(seeds[11], 71), 0)
    elem_live = draw_elem_live(jax.random.fold_in(seeds[11], 71), 0)
    currents = gaussian(seeds[5], (BLOCKS, BS, NRHS), 0.03, 0.1796875, ((0, 128),))
    positions = draw_positions(jax.random.fold_in(seeds[11], 71), 0)
    block_live = touch_ends(jax.random.randint(seeds[7], (BLOCKS,), BS // 4, BS + 1), jax.random.fold_in(seeds[7], 1), BS // 4, BS).astype(jnp.int32)
    block_owner = draw_block_owner(jax.random.fold_in(seeds[11], 71), 0)
    block_leaf = touch_ends(jax.random.randint(seeds[9], (BLOCKS,), 0, LEAVES_DEV), jax.random.fold_in(seeds[9], 1), 0, LEAVES_DEV - 1).astype(jnp.int32)
    cone_waves = draw_cone_waves(jax.random.fold_in(seeds[11], 71), 0)
    return {"x_edges": x_edges, "send_list": send_list, "connectivity": connectivity, "elem_mats": elem_mats, "elem_live": elem_live, "currents": currents, "positions": positions, "block_live": block_live, "block_owner": block_owner, "block_leaf": block_leaf, "cone_waves": cone_waves}


def cheb_points():
    node_order = jnp.arange(NODES).astype(jnp.float32)
    return jnp.cos((2.0 * node_order + 1.0) * (jnp.pi / (2.0 * NODES)))


def lagrange(points):
    node_values = cheb_points()
    rows_out = []
    for target in range(NODES):
        product = jnp.ones_like(points)
        for other_node in range(NODES):
            if other_node != target:
                product = product * (points - node_values[other_node]) / (node_values[target] - node_values[other_node])
        rows_out.append(product)
    return jnp.stack(rows_out, axis=-2)


def tensor_basis(coords):
    first = lagrange(coords[..., 0, :])
    second = lagrange(coords[..., 1, :])
    third = lagrange(coords[..., 2, :])
    joined = first[..., :, None, None, :] * second[..., None, :, None, :] * third[..., None, None, :, :]
    return joined.reshape(coords.shape[:-2] + (NODES ** 3, coords.shape[-1]))


def node_coords():
    ladder = jnp.arange(NODES ** 3)
    digits = jnp.stack([ladder // (NODES * NODES), (ladder // NODES) % NODES, ladder % NODES]).astype(jnp.float32)
    return jnp.cos((2.0 * digits + 1.0) * (jnp.pi / (2.0 * NODES)))


def wave_phase(waves, coords):
    return (waves[0][:, None] * coords[..., None, 0, :] + waves[1][:, None] * coords[..., None, 1, :]
            + waves[2][:, None] * coords[..., None, 2, :])


def m2m_tables(waves):
    octant = jnp.arange(8)
    shifts = jnp.stack([octant // 4, (octant // 2) % 2, octant % 2], axis=1).astype(jnp.float32) - 0.5
    points = shifts[:, :, None] + 0.5 * cheb_points()[None, None, :]
    weights = lagrange(points)
    first = weights[:, 0]
    second = weights[:, 1]
    third = weights[:, 2]
    joined = first[:, :, None, None, :, None, None] * second[:, None, :, None, None, :, None] * third[:, None, None, :, None, None, :]
    square = NODES ** 3
    joined = joined.reshape(8, square, square)
    child = shifts[:, :, None] + 0.5 * node_coords()[None]
    spread = child[:, :, None, :] - node_coords()[None, :, :, None]
    psi = 2.0 * (waves[0][:, None, None, None] * spread[None, :, 0] + waves[1][:, None, None, None] * spread[None, :, 1]
                 + waves[2][:, None, None, None] * spread[None, :, 2])
    table_real = (joined[None] * jnp.cos(psi)).astype(jnp.bfloat16)
    table_imag = (-joined[None] * jnp.sin(psi)).astype(jnp.bfloat16)
    return table_real, table_imag


def interior_product(x_edges, send_list, connectivity, elem_mats, elem_live):
    total_rows = x_edges.shape[0]
    columns = x_edges.shape[1]

    def one_part(accumulated, device):
        local_links = lax.dynamic_slice_in_dim(connectivity, device * EL_DEV, EL_DEV, 1)
        matrices = lax.dynamic_slice_in_dim(elem_mats, device * EL_DEV, EL_DEV, 1)
        offset = jnp.maximum(local_links - E_OWN, 0)
        sender = offset // HS
        listed = send_list[sender * PARTITIONS + device, offset % HS]
        global_rows = jnp.where(local_links < E_OWN, device * E_OWN + local_links, sender * E_OWN + listed).astype(jnp.int32)
        gathered = x_edges[global_rows]
        live_mask = (jnp.arange(EL_DEV) < elem_live[device])[:, None]
        term_list = []
        for row_index in range(6):
            summed = jnp.zeros((EL_DEV, columns), jnp.float32)
            for col_index in range(6):
                summed = summed + matrices[row_index * 6 + col_index][:, None] * gathered[col_index].astype(jnp.float32)
            term_list.append(jnp.where(live_mask, summed, jnp.zeros_like(summed)))
        stacked = jnp.stack(term_list).reshape(6 * EL_DEV, columns)
        return accumulated.at[global_rows.reshape(-1)].add(stacked), None

    initial = jnp.zeros((total_rows, columns), jnp.float32)
    result, unused = lax.scan(one_part, initial, jnp.arange(PARTITIONS, dtype=jnp.int32))
    return result


def boundary_product(currents, positions, block_live, block_owner, block_leaf, cone_waves):
    cone_total = cone_waves.shape[1]
    columns = currents.shape[2]
    square = NODES ** 3
    live_mask = jnp.arange(BS)[None, :] < block_live[:, None]
    masked = jnp.where(live_mask[:, :, None], currents, jnp.zeros_like(currents))
    leaf_index = (block_owner * LEAVES_DEV + block_leaf).astype(jnp.int32)
    batches = BLOCKS // 128

    def one_batch(carry, inputs):
        real_sum, imag_sum = carry
        blocks_now, coords, leaves = inputs
        coords_wide = coords.astype(jnp.float32)
        basis_now = tensor_basis(coords_wide)
        phase_now = wave_phase(cone_waves, coords_wide)
        real_w = (basis_now[:, None] * jnp.cos(phase_now)[:, :, None, :]).astype(jnp.bfloat16)
        imag_w = (-basis_now[:, None] * jnp.sin(phase_now)[:, :, None, :]).astype(jnp.bfloat16)
        block_data = blocks_now.astype(jnp.float32)
        real_part = jnp.einsum("gcqb,gbn->gcqn", real_w.astype(jnp.float32), block_data).astype(jnp.bfloat16)
        imag_part = jnp.einsum("gcqb,gbn->gcqn", imag_w.astype(jnp.float32), block_data).astype(jnp.bfloat16)
        real_sum = real_sum.at[leaves].add(real_part.astype(jnp.float32))
        imag_sum = imag_sum.at[leaves].add(imag_part.astype(jnp.float32))
        return (real_sum, imag_sum), None

    empty = jnp.zeros((LEAVES, cone_total, square, columns), jnp.float32)
    inputs = (masked.reshape(batches, 128, BS, columns), positions.reshape(batches, 128, 3, BS), leaf_index.reshape(batches, 128))
    sums, unused = lax.scan(one_batch, (empty, empty), inputs)
    real_sum, imag_sum = sums
    node_phase = wave_phase(cone_waves, node_coords())
    cosine = jnp.cos(node_phase)[None, :, :, None]
    sine_part = jnp.sin(node_phase)[None, :, :, None]
    leaf_real = (cosine * real_sum - sine_part * imag_sum).astype(jnp.bfloat16)
    leaf_imag = (cosine * imag_sum + sine_part * real_sum).astype(jnp.bfloat16)
    table_real, table_imag = m2m_tables(cone_waves)
    child_real = leaf_real.reshape(LEAVES // 8, 8, cone_total, square, columns).astype(jnp.float32)
    child_imag = leaf_imag.reshape(LEAVES // 8, 8, cone_total, square, columns).astype(jnp.float32)
    wide_real = table_real.astype(jnp.float32)
    wide_imag = table_imag.astype(jnp.float32)
    parent_real = jnp.einsum("cops,xocsn->xcpn", wide_real, child_real) - jnp.einsum("cops,xocsn->xcpn", wide_imag, child_imag)
    parent_imag = jnp.einsum("cops,xocsn->xcpn", wide_real, child_imag) + jnp.einsum("cops,xocsn->xcpn", wide_imag, child_real)
    return jnp.stack([parent_real, parent_imag], axis=2)


def reference(x_edges, send_list, connectivity, elem_mats, elem_live, currents, positions, block_live, block_owner, block_leaf, cone_waves):
    interior_out = interior_product(x_edges, send_list, connectivity, elem_mats, elem_live)
    expansions = boundary_product(currents, positions, block_live, block_owner, block_leaf, cone_waves)
    return (interior_out, expansions)
```

```python
import functools
import math

import jax
import jax.numpy as jnp
from jax import lax
from jax.experimental import pallas as pl
from jax.experimental.pallas import tpu as pltpu
from jax.sharding import PartitionSpec as P

NODES = 4
SQUARE = NODES**3
DIRS = 4
ROWS = 136
VMEM_LIMIT = 60 * 1024 * 1024
NODE_T = [math.cos((2 * j + 1) * math.pi / (2 * NODES)) for j in range(NODES)]


def vmem():
    return pl.BlockSpec(memory_space=pltpu.VMEM)


def smem():
    return pl.BlockSpec(memory_space=pltpu.SMEM)


def params():
    return pltpu.CompilerParams(vmem_limit_bytes=VMEM_LIMIT)


def pick_kernel(list_ref, x_ref, out_ref, wide, picked):
    owned, columns = x_ref.shape
    count, width = list_ref.shape
    wide[0:owned, :] = x_ref[...].astype(jnp.float32)
    wide[owned : owned + 8, :] = jnp.zeros((8, columns), jnp.float32)

    def one(row, carry):
        for slot in range(width):
            picked[pl.ds(row * width + slot, 1), :] = wide[pl.ds(list_ref[row, slot], 1), :]
        return carry

    lax.fori_loop(0, count, one, 0)
    out_ref[...] = picked[...].astype(out_ref.dtype)


def pick_rows(send_list, x_edges):
    owned, columns = x_edges.shape
    total = send_list.shape[0] * send_list.shape[1]
    return pl.pallas_call(
        pick_kernel,
        out_shape=jax.ShapeDtypeStruct((total, columns), x_edges.dtype),
        in_specs=[smem(), vmem()],
        out_specs=vmem(),
        scratch_shapes=[
            pltpu.VMEM((owned + 8, columns), jnp.float32),
            pltpu.VMEM((total, columns), jnp.float32),
        ],
        compiler_params=params(),
        cost_estimate=pl.CostEstimate(flops=0, bytes_accessed=1 << 24, transcendentals=0),
        name="pick_rows",
    )(send_list, x_edges)


GROUP = 8
PAIR = 2


def element_kernel(
    conn_ref, x_ref, halo_ref, mats_ref, local_ref, back_ref, table, stage, terms, *sums
):
    owned = x_ref.shape[0]
    halo = halo_ref.shape[0]
    elements = conn_ref.shape[1]
    columns = x_ref.shape[1]
    table[0:owned, :] = x_ref[...].astype(jnp.float32)
    table[owned : owned + halo, :] = halo_ref[...].astype(jnp.float32)
    for total in sums:
        total[...] = jnp.zeros_like(total)
    split = len(sums)

    def one(step, carry):
        for part in range(PAIR):
            first = (step * PAIR + part) * GROUP
            base = part * 6 * GROUP
            for j in range(6):
                for s in range(GROUP):
                    stage[base + j * GROUP + s : base + j * GROUP + s + 1, :] = table[
                        pl.ds(conn_ref[j, first + s], 1), :
                    ]
        for part in range(PAIR):
            first = (step * PAIR + part) * GROUP
            base = part * 6 * GROUP
            coefs = mats_ref[pl.ds(pl.multiple_of(first, GROUP), GROUP), :]
            values = [stage[base + j * GROUP : base + (j + 1) * GROUP, :] for j in range(6)]
            for i in range(6):
                term = None
                for j in range(6):
                    q = i * 6 + j
                    piece = jnp.broadcast_to(coefs[:, q : q + 1], (GROUP, columns)) * values[j]
                    term = piece if term is None else term + piece
                terms[base + i * GROUP : base + (i + 1) * GROUP, :] = term
        for part in range(PAIR):
            first = (step * PAIR + part) * GROUP
            base = part * 6 * GROUP
            for s in range(GROUP):
                for i in range(6):
                    row = pl.ds(conn_ref[i, first + s], 1)
                    at = base + i * GROUP + s
                    total = sums[i % split]
                    total[row, :] = total[row, :] + terms[at : at + 1, :]
        return carry

    lax.fori_loop(0, elements // (GROUP * PAIR), one, 0)

    def finish(step, carry):
        at = pl.ds(pl.multiple_of(step * 256, 256), 256)
        whole = sums[0][at, :]
        for total in sums[1:]:
            whole = whole + total[at, :]
        local_ref[at, :] = whole
        return carry

    lax.fori_loop(0, owned // 256, finish, 0)

    def finish_back(step, carry):
        at = pl.ds(pl.multiple_of(step * 256, 256), 256)
        src = pl.ds(pl.multiple_of(owned + step * 256, 256), 256)
        whole = sums[0][src, :]
        for total in sums[1:]:
            whole = whole + total[src, :]
        back_ref[at, :] = whole.astype(back_ref.dtype)
        return carry

    lax.fori_loop(0, halo // 256, finish_back, 0)


def element_sums(connectivity, x_edges, halo, mats):
    owned, columns = x_edges.shape
    slots = halo.shape[0]
    return pl.pallas_call(
        element_kernel,
        out_shape=(
            jax.ShapeDtypeStruct((owned, columns), jnp.float32),
            jax.ShapeDtypeStruct((slots, columns), jnp.bfloat16),
        ),
        in_specs=[smem(), vmem(), vmem(), vmem()],
        out_specs=(vmem(), vmem()),
        scratch_shapes=[
            pltpu.VMEM((owned + slots, columns), jnp.float32),
            pltpu.VMEM((6 * GROUP * PAIR, columns), jnp.float32),
            pltpu.VMEM((6 * GROUP * PAIR, columns), jnp.float32),
        ]
        + [pltpu.VMEM((owned + slots, columns), jnp.float32) for _ in range(6)],
        compiler_params=params(),
        cost_estimate=pl.CostEstimate(flops=0, bytes_accessed=1 << 26, transcendentals=0),
        name="element_sums",
    )(connectivity, x_edges, halo, mats)


def fold_kernel(list_ref, returned_ref, local_ref, out_ref):
    owned = local_ref.shape[0]
    total = returned_ref.shape[0]
    tile = 256

    def one(step, carry):
        at = pl.ds(pl.multiple_of(step * tile, tile), tile)
        rows = lax.broadcasted_iota(jnp.int32, (tile, total), 0) + step * tile
        hot = jnp.where(rows == list_ref[...], 1.0, 0.0).astype(jnp.bfloat16)
        out_ref[at, :] = local_ref[at, :] + jnp.dot(
            hot, returned_ref[...], preferred_element_type=jnp.float32
        )
        return carry

    lax.fori_loop(0, owned // tile, one, 0)


def fold_back(list_row, returned, local):
    return pl.pallas_call(
        fold_kernel,
        out_shape=jax.ShapeDtypeStruct(local.shape, jnp.float32),
        in_specs=[vmem(), vmem(), vmem()],
        out_specs=vmem(),
        compiler_params=params(),
        cost_estimate=pl.CostEstimate(flops=0, bytes_accessed=1 << 24, transcendentals=0),
        name="fold_back",
    )(list_row, returned, local)


def sin_cos_turns(turns):
    reduced = turns - jnp.floor(turns + 0.5)
    half = reduced * math.pi
    square = half * half

    def series(coefs):
        total = jnp.full_like(square, coefs[-1])
        for coef in coefs[-2::-1]:
            total = total * square + coef
        return total

    sine = half * series([(-1) ** n / math.factorial(2 * n + 1) for n in range(6)])
    cosine = series([(-1) ** n / math.factorial(2 * n) for n in range(7)])
    return 2.0 * sine * cosine, 1.0 - 2.0 * sine * sine


def digit_polynomial(coords, digit):
    total = None
    for j in range(NODES):
        value = None
        for i in range(NODES):
            if i != j:
                factor = (coords - NODE_T[i]) * (1.0 / (NODE_T[j] - NODE_T[i]))
                value = factor if value is None else value * factor
        total = value if total is None else jnp.where(digit == j, value, total)
    return total


def parent_kernel(blocks_ref, waves_ref, *refs):
    outs = refs[:DIRS]
    weights, sources, sums = refs[DIRS:]
    slots, unused, columns = blocks_ref.shape
    cones = waves_ref.shape[1]
    size = columns
    per_dir = cones // DIRS
    span = sources.shape[0] // size

    lane_rows = lax.broadcasted_iota(jnp.int32, (8, size), 0)
    y_rows = lax.broadcasted_iota(jnp.int32, (size, columns), 0).astype(jnp.float32)
    third_digit = lane_rows % NODES
    second_low = lane_rows // NODES

    sums[...] = jnp.zeros_like(sums)

    def one(step, carry):
        for part in range(span):
            slot = step * span + part
            meta = blocks_ref[slot, size : size + 8, :].astype(jnp.float32)
            block = blocks_ref[slot, 0:size, :].astype(jnp.float32)
            live = jnp.broadcast_to(meta[7:8, :], (size, columns))
            parent = jnp.broadcast_to(meta[6:7, :], (size, columns))
            block = jnp.where(y_rows < live, block, 0.0)
            at = slice(part * size, (part + 1) * size)
            sources[at, 0:columns] = jnp.where(parent < 0.5, block, 0.0).astype(jnp.bfloat16)
            sources[at, columns : 2 * columns] = jnp.where(parent > 0.5, block, 0.0).astype(
                jnp.bfloat16
            )
            shifted = meta[0:3, :] + meta[3:6, :]
            turns = None
            for d in range(3):
                piece = waves_ref[d] * jnp.broadcast_to(shifted[d : d + 1, :], (cones, size))
                turns = piece if turns is None else turns + piece
            sine, cosine = sin_cos_turns(turns)
            coords = shifted * 0.5
            along = [jnp.broadcast_to(coords[d : d + 1, :], (8, size)) for d in range(3)]
            third = digit_polynomial(along[2], third_digit)
            second = [digit_polynomial(along[1], second_low + 2 * h) * third for h in range(2)]
            first = [
                digit_polynomial(along[0], jnp.full((8, size), j, jnp.int32)) for j in range(NODES)
            ]
            basis = jnp.concatenate([first[v // 2] * second[v % 2] for v in range(8)], axis=0)
            for k in range(cones):
                base = k * 2 * SQUARE
                weights[base : base + SQUARE, at] = (
                    basis * jnp.broadcast_to(cosine[k : k + 1, :], (SQUARE, size))
                ).astype(jnp.bfloat16)
                weights[base + SQUARE : base + 2 * SQUARE, at] = (
                    basis * jnp.broadcast_to(-sine[k : k + 1, :], (SQUARE, size))
                ).astype(jnp.bfloat16)
        height = 512
        for row in range(0, cones * 2 * SQUARE, height):
            sums[row : row + height, :] += jnp.dot(
                weights[row : row + height, :],
                sources[...],
                preferred_element_type=jnp.float32,
            )
        return carry

    lax.fori_loop(0, slots // span, one, 0)

    node_rows = lax.broadcasted_iota(jnp.int32, (SQUARE, columns), 0)

    def node_value(digit):
        value = jnp.full((SQUARE, columns), NODE_T[0], jnp.float32)
        for j in range(1, NODES):
            value = jnp.where(digit == j, NODE_T[j], value)
        return value

    nodes = [
        node_value(node_rows // (NODES * NODES)),
        node_value(node_rows // NODES % NODES),
        node_value(node_rows % NODES),
    ]
    for k in range(cones):
        turns = None
        for d in range(3):
            wave = jnp.broadcast_to(waves_ref[d, k : k + 1, :], (SQUARE, columns))
            piece = wave * nodes[d]
            turns = piece if turns is None else turns + piece
        sine, cosine = sin_cos_turns(2.0 * turns)
        base = k * 2 * SQUARE
        out = outs[k // per_dir]
        for p in range(2):
            cols = slice(p * columns, (p + 1) * columns)
            real = sums[base : base + SQUARE, cols]
            imag = sums[base + SQUARE : base + 2 * SQUARE, cols]
            out[p, k % per_dir, 0] = (cosine * real - sine * imag).astype(out.dtype)
            out[p, k % per_dir, 1] = (cosine * imag + sine * real).astype(out.dtype)


SPAN = 2


def parent_sums(blocks, waves):
    columns = blocks.shape[2]
    cones = waves.shape[1]
    piece = (2, cones // DIRS, 2, SQUARE, columns)
    rows = cones * 2 * SQUARE
    return pl.pallas_call(
        parent_kernel,
        out_shape=(jax.ShapeDtypeStruct(piece, jnp.float32),)
        + (jax.ShapeDtypeStruct(piece, jnp.bfloat16),) * (DIRS - 1),
        in_specs=[vmem(), vmem()],
        out_specs=(vmem(),) * DIRS,
        scratch_shapes=[
            pltpu.VMEM((rows, SPAN * 128), jnp.bfloat16),
            pltpu.VMEM((SPAN * 128, 2 * columns), jnp.bfloat16),
            pltpu.VMEM((rows, 2 * columns), jnp.float32),
        ],
        compiler_params=params(),
        cost_estimate=pl.CostEstimate(
            flops=2 * rows * 2 * columns * blocks.shape[0] * 128,
            bytes_accessed=1 << 24,
            transcendentals=0,
        ),
        name="parent_sums",
    )(blocks, waves)


def packed_blocks(currents, positions, block_live, block_owner, block_leaf):
    count, size, columns = currents.shape
    owners = lax.axis_size("dom")
    capacity = 3 * count // owners
    octant = block_leaf % 8
    digits = jnp.stack([octant // 4, octant // 2 % 2, octant % 2], axis=1)
    facts = jnp.concatenate(
        [2 * digits - 1, (block_leaf // 8)[:, None], block_live[:, None]], axis=1
    ).astype(jnp.bfloat16)
    joined = jnp.concatenate(
        [currents, positions, jnp.broadcast_to(facts[:, :, None], (count, 5, columns))], axis=1
    )
    joined = jnp.concatenate([joined, jnp.zeros((1, ROWS, columns), joined.dtype)])
    order = jnp.arange(count)
    same = (block_owner[:, None] == block_owner[None, :]) & (order[None, :] < order[:, None])
    slot = block_owner * capacity + jnp.sum(same.astype(jnp.int32), axis=1)
    hits = slot[None, :] == jnp.arange(owners * capacity)[:, None]
    source = jnp.min(jnp.where(hits, order[None, :], count), axis=1)
    return joined[source]


def shards(
    x_edges,
    send_list,
    connectivity,
    elem_mats,
    elem_live,
    currents,
    positions,
    block_live,
    block_owner,
    block_leaf,
    cone_waves,
):
    owned, columns = x_edges.shape
    partitions, width = send_list.shape
    elements = connectivity.shape[1]
    everywhere = ("dom", "dir")

    outgoing = pick_rows(send_list, x_edges).reshape(partitions, width, columns)
    halo = lax.all_to_all(outgoing, everywhere, split_axis=0, concat_axis=0, tiled=True)

    waves = [cone_waves]
    for s in range(1, DIRS):
        waves.append(
            lax.ppermute(cone_waves, "dir", [(i, (i - s) % DIRS) for i in range(DIRS)])
        )
    waves = jnp.concatenate(waves, axis=1) * (0.5 / math.pi)
    waves = jnp.broadcast_to(waves[:, :, None], waves.shape + (columns,))

    packed = packed_blocks(currents, positions, block_live, block_owner, block_leaf)
    live = jnp.arange(elements)[None, :] < elem_live[0]
    mats = jnp.where(live, elem_mats, 0.0).T
    list_row = send_list.reshape(1, partitions * width)

    halo, packed, mats, list_row = lax.optimization_barrier((halo, packed, mats, list_row))
    arrived = lax.all_to_all(packed, "dom", split_axis=0, concat_axis=0, tiled=True)
    local, back = element_sums(
        connectivity, x_edges, halo.reshape(partitions * width, columns), mats
    )
    back, arrived = lax.optimization_barrier((back, arrived))
    returned = lax.all_to_all(
        back.reshape(partitions, width, columns),
        everywhere,
        split_axis=0,
        concat_axis=0,
        tiled=True,
    )
    pieces = parent_sums(arrived, waves)
    expansions = pieces[0]
    for s in range(1, DIRS):
        moved = lax.ppermute(pieces[s], "dir", [(i, (i + s) % DIRS) for i in range(DIRS)])
        expansions = expansions + moved.astype(jnp.float32)
    interior_out = fold_back(list_row, returned.reshape(partitions * width, columns), local)
    return (interior_out, expansions)


def solution(mesh):
    both = ("dom", "dir")
    placed = (
        P(both, None),
        P(both, None),
        P(None, both),
        P(None, both),
        P(both),
        P(both, None, None),
        P(both, None, None),
        P(both),
        P(both),
        P(both),
        P(None, "dir"),
    )
    return jax.shard_map(
        shards,
        mesh=mesh,
        in_specs=placed,
        out_specs=(P(both, None), P("dom", "dir", None, None, None)),
        check_vma=False,
    )
```

```python
import functools
import math

import jax
import jax.numpy as jnp
from jax import lax
from jax.experimental import pallas as pl
from jax.experimental.pallas import tpu as pltpu
from jax.sharding import PartitionSpec as P

NODES = 4
SQUARE = NODES**3
DIRS = 4
ROWS = 136
VMEM_LIMIT = 60 * 1024 * 1024
NODE_T = [math.cos((2 * j + 1) * math.pi / (2 * NODES)) for j in range(NODES)]


def vmem():
    return pl.BlockSpec(memory_space=pltpu.VMEM)


def smem():
    return pl.BlockSpec(memory_space=pltpu.SMEM)


def params():
    return pltpu.CompilerParams(vmem_limit_bytes=VMEM_LIMIT)


def pick_kernel(list_ref, x_ref, out_ref, flipped):
    owned, columns = x_ref.shape
    total = list_ref.shape[1]
    tile = min(1024, total)
    flipped[...] = x_ref[...].T

    def one(step, carry):
        at = pl.ds(pl.multiple_of(step * tile, tile), tile)
        rows = lax.broadcasted_iota(jnp.int32, (owned, tile), 0)
        hot = jnp.where(rows == list_ref[:, at], 1.0, 0.0).astype(flipped.dtype)
        picked = jnp.dot(flipped[...], hot, preferred_element_type=jnp.float32)
        out_ref[at, :] = picked.T.astype(out_ref.dtype)
        return carry

    lax.fori_loop(0, total // tile, one, 0)


def pick_rows(list_row, x_edges):
    owned, columns = x_edges.shape
    total = list_row.shape[1]
    return pl.pallas_call(
        pick_kernel,
        out_shape=jax.ShapeDtypeStruct((total, columns), x_edges.dtype),
        in_specs=[vmem(), vmem()],
        out_specs=vmem(),
        scratch_shapes=[pltpu.VMEM((columns, owned), x_edges.dtype)],
        compiler_params=params(),
        cost_estimate=pl.CostEstimate(flops=0, bytes_accessed=1 << 24, transcendentals=0),
        name="pick_rows",
    )(list_row, x_edges)


GROUP = 8
PAIR = 2


def element_kernel(
    conn_ref, x_ref, halo_ref, mats_ref, local_ref, back_ref, table, stage, terms, *sums
):
    owned = x_ref.shape[0]
    halo = halo_ref.shape[0]
    elements = conn_ref.shape[1]
    columns = x_ref.shape[1]
    table[0:owned, :] = x_ref[...].astype(jnp.float32)
    table[owned : owned + halo, :] = halo_ref[...].astype(jnp.float32)
    for total in sums:
        total[...] = jnp.zeros_like(total)
    split = len(sums)

    def one(step, carry):
        for part in range(PAIR):
            first = (step * PAIR + part) * GROUP
            base = part * 6 * GROUP
            for j in range(6):
                for s in range(GROUP):
                    stage[base + j * GROUP + s : base + j * GROUP + s + 1, :] = table[
                        pl.ds(conn_ref[j, first + s], 1), :
                    ]
        for part in range(PAIR):
            first = (step * PAIR + part) * GROUP
            base = part * 6 * GROUP
            coefs = mats_ref[pl.ds(pl.multiple_of(first, GROUP), GROUP), :]
            values = [stage[base + j * GROUP : base + (j + 1) * GROUP, :] for j in range(6)]
            for i in range(6):
                term = None
                for j in range(6):
                    q = i * 6 + j
                    piece = jnp.broadcast_to(coefs[:, q : q + 1], (GROUP, columns)) * values[j]
                    term = piece if term is None else term + piece
                terms[base + i * GROUP : base + (i + 1) * GROUP, :] = term
        for part in range(PAIR):
            first = (step * PAIR + part) * GROUP
            base = part * 6 * GROUP
            for s in range(GROUP):
                for i in range(6):
                    row = pl.ds(conn_ref[i, first + s], 1)
                    at = base + i * GROUP + s
                    total = sums[i % split]
                    total[row, :] = total[row, :] + terms[at : at + 1, :]
        return carry

    lax.fori_loop(0, elements // (GROUP * PAIR), one, 0)

    def finish(step, carry):
        at = pl.ds(pl.multiple_of(step * 256, 256), 256)
        whole = sums[0][at, :]
        for total in sums[1:]:
            whole = whole + total[at, :]
        local_ref[at, :] = whole
        return carry

    lax.fori_loop(0, owned // 256, finish, 0)

    def finish_back(step, carry):
        at = pl.ds(pl.multiple_of(step * 256, 256), 256)
        src = pl.ds(pl.multiple_of(owned + step * 256, 256), 256)
        whole = sums[0][src, :]
        for total in sums[1:]:
            whole = whole + total[src, :]
        back_ref[at, :] = whole.astype(back_ref.dtype)
        return carry

    lax.fori_loop(0, halo // 256, finish_back, 0)


def element_sums(connectivity, x_edges, halo, mats):
    owned, columns = x_edges.shape
    slots = halo.shape[0]
    return pl.pallas_call(
        element_kernel,
        out_shape=(
            jax.ShapeDtypeStruct((owned, columns), jnp.float32),
            jax.ShapeDtypeStruct((slots, columns), jnp.bfloat16),
        ),
        in_specs=[smem(), vmem(), vmem(), vmem()],
        out_specs=(vmem(), vmem()),
        scratch_shapes=[
            pltpu.VMEM((owned + slots, columns), jnp.float32),
            pltpu.VMEM((6 * GROUP * PAIR, columns), jnp.float32),
            pltpu.VMEM((6 * GROUP * PAIR, columns), jnp.float32),
        ]
        + [pltpu.VMEM((owned + slots, columns), jnp.float32) for _ in range(6)],
        compiler_params=params(),
        cost_estimate=pl.CostEstimate(flops=0, bytes_accessed=1 << 26, transcendentals=0),
        name="element_sums",
    )(connectivity, x_edges, halo, mats)


def fold_kernel(list_ref, returned_ref, local_ref, out_ref, flipped):
    owned, columns = local_ref.shape
    tile = FOLD_TILE
    flipped[...] = returned_ref[...].T
    lanes = lax.broadcasted_iota(jnp.int32, list_ref.shape, 1)

    def one(step, carry):
        hots = []
        for part in range(tile // columns):
            want = lanes + (step * tile + part * columns)
            hots.append(jnp.where(list_ref[...] == want, 1.0, 0.0).astype(flipped.dtype))
        total = jnp.dot(
            flipped[...], jnp.concatenate(hots, axis=1), preferred_element_type=jnp.float32
        )
        at = pl.ds(pl.multiple_of(step * tile, tile), tile)
        out_ref[at, :] = local_ref[at, :] + total.T
        return carry

    lax.fori_loop(0, owned // tile, one, 0)


FOLD_TILE = 512


def fold_back(list_lanes, returned, local):
    return pl.pallas_call(
        fold_kernel,
        out_shape=jax.ShapeDtypeStruct(local.shape, jnp.float32),
        in_specs=[vmem(), vmem(), vmem()],
        out_specs=vmem(),
        scratch_shapes=[pltpu.VMEM(returned.shape[::-1], returned.dtype)],
        compiler_params=params(),
        cost_estimate=pl.CostEstimate(flops=1 << 32, bytes_accessed=1 << 24, transcendentals=0),
        name="fold_back",
    )(list_lanes, returned, local)


def sin_cos_turns(turns):
    reduced = turns - jnp.floor(turns + 0.5)
    half = reduced * math.pi
    square = half * half

    def series(coefs):
        total = jnp.full_like(square, coefs[-1])
        for coef in coefs[-2::-1]:
            total = total * square + coef
        return total

    sine = half * series([(-1) ** n / math.factorial(2 * n + 1) for n in range(6)])
    cosine = series([(-1) ** n / math.factorial(2 * n) for n in range(7)])
    return 2.0 * sine * cosine, 1.0 - 2.0 * sine * sine


def node_polynomials(coords):
    away = [coords - t for t in NODE_T]
    low, high = away[0] * away[1], away[2] * away[3]
    pairs = [away[1] * high, away[0] * high, low * away[3], low * away[2]]
    scaled = []
    for j in range(NODES):
        scale = math.prod(NODE_T[j] - NODE_T[i] for i in range(NODES) if i != j)
        scaled.append(pairs[j] * (1.0 / scale))
    return scaled


def parent_kernel(blocks_ref, waves_ref, *refs):
    outs, (weights, sources, sums) = refs[:-3], refs[-3:]
    slots, unused, columns = blocks_ref.shape
    cones = waves_ref.shape[1]
    size = columns
    per_dir = cones // len(outs)
    span = sources.shape[0] // size

    sub = lax.broadcasted_iota(jnp.int32, (8, size), 0)
    y_rows = lax.broadcasted_iota(jnp.int32, (size, columns), 0).astype(jnp.float32)
    y_rows = y_rows.astype(jnp.bfloat16)
    zero = jnp.zeros((size, columns), jnp.bfloat16)

    sums[...] = jnp.zeros_like(sums)

    def one(step, carry):
        for part in range(span):
            slot = step * span + part
            tail = blocks_ref[slot, size : size + 8, :]
            live = jnp.broadcast_to(tail[7:8, :], (size, columns))
            parent = jnp.broadcast_to(tail[6:7, :], (size, columns))
            block = jnp.where(y_rows < live, blocks_ref[slot, 0:size, :], zero)
            at = slice(part * size, (part + 1) * size)
            second_parent = parent > jnp.bfloat16(0.5)
            sources[at, 0:columns] = jnp.where(second_parent, zero, block)
            sources[at, columns : 2 * columns] = jnp.where(second_parent, block, zero)
            meta = tail.astype(jnp.float32)
            shifted = meta[0:3, :] + meta[3:6, :]
            turns = None
            for d in range(3):
                piece = waves_ref[d] * jnp.broadcast_to(shifted[d : d + 1, :], (cones, size))
                turns = piece if turns is None else turns + piece
            sine, cosine = sin_cos_turns(turns)
            along = node_polynomials(shifted * 0.5)

            def row(d, j):
                return jnp.broadcast_to(along[j][d : d + 1, :], (8, size))

            third = row(2, 3)
            for j in range(NODES - 1):
                third = jnp.where(sub % NODES == j, row(2, j), third)
            second = [
                jnp.where(sub < NODES, row(1, 2 * h), row(1, 2 * h + 1)) * third for h in range(2)
            ]
            first = [row(0, j) for j in range(NODES)]
            basis = jnp.concatenate([first[v // 2] * second[v % 2] for v in range(8)], axis=0)
            for k in range(cones):
                base = k * 2 * SQUARE
                weights[base : base + SQUARE, at] = (
                    basis * jnp.broadcast_to(cosine[k : k + 1, :], (SQUARE, size))
                ).astype(jnp.bfloat16)
                weights[base + SQUARE : base + 2 * SQUARE, at] = (
                    basis * jnp.broadcast_to(-sine[k : k + 1, :], (SQUARE, size))
                ).astype(jnp.bfloat16)
        height = min(512, cones * 2 * SQUARE)
        for row in range(0, cones * 2 * SQUARE, height):
            sums[row : row + height, :] += jnp.dot(
                weights[row : row + height, :],
                sources[...],
                preferred_element_type=jnp.float32,
            )
        return carry

    lax.fori_loop(0, slots // span, one, 0)

    node_rows = lax.broadcasted_iota(jnp.int32, (SQUARE, columns), 0)

    def node_value(digit):
        value = jnp.full((SQUARE, columns), NODE_T[0], jnp.float32)
        for j in range(1, NODES):
            value = jnp.where(digit == j, NODE_T[j], value)
        return value

    nodes = [
        node_value(node_rows // (NODES * NODES)),
        node_value(node_rows // NODES % NODES),
        node_value(node_rows % NODES),
    ]
    for k in range(cones):
        turns = None
        for d in range(3):
            wave = jnp.broadcast_to(waves_ref[d, k : k + 1, :], (SQUARE, columns))
            piece = wave * nodes[d]
            turns = piece if turns is None else turns + piece
        sine, cosine = sin_cos_turns(2.0 * turns)
        base = k * 2 * SQUARE
        out = outs[k // per_dir]
        for p in range(2):
            cols = slice(p * columns, (p + 1) * columns)
            real = sums[base : base + SQUARE, cols]
            imag = sums[base + SQUARE : base + 2 * SQUARE, cols]
            out[p, k % per_dir, 0] = (cosine * real - sine * imag).astype(out.dtype)
            out[p, k % per_dir, 1] = (cosine * imag + sine * real).astype(out.dtype)


SPAN = 8


def parent_sums(blocks, waves, dtypes):
    columns = blocks.shape[2]
    cones = waves.shape[1]
    piece = (2, cones // len(dtypes), 2, SQUARE, columns)
    rows = cones * 2 * SQUARE
    return pl.pallas_call(
        parent_kernel,
        out_shape=tuple(jax.ShapeDtypeStruct(piece, dtype) for dtype in dtypes),
        in_specs=[vmem(), vmem()],
        out_specs=(vmem(),) * len(dtypes),
        scratch_shapes=[
            pltpu.VMEM((rows, SPAN * columns), jnp.bfloat16),
            pltpu.VMEM((SPAN * columns, 2 * columns), jnp.bfloat16),
            pltpu.VMEM((rows, 2 * columns), jnp.float32),
        ],
        compiler_params=params(),
        cost_estimate=pl.CostEstimate(
            flops=2 * rows * 2 * columns * blocks.shape[0] * columns,
            bytes_accessed=1 << 23,
            transcendentals=0,
        ),
        name="parent_sums",
    )(blocks, waves)


def packed_blocks(currents, positions, block_live, block_owner, block_leaf):
    count, size, columns = currents.shape
    owners = lax.axis_size("dom")
    capacity = 3 * count // owners
    octant = block_leaf % 8
    digits = jnp.stack([octant // 4, octant // 2 % 2, octant % 2], axis=1)
    facts = jnp.concatenate(
        [2 * digits - 1, (block_leaf // 8)[:, None], block_live[:, None]], axis=1
    ).astype(jnp.bfloat16)
    joined = jnp.concatenate(
        [currents, positions, jnp.broadcast_to(facts[:, :, None], (count, 5, columns))], axis=1
    )
    joined = jnp.concatenate([joined, jnp.zeros((1, ROWS, columns), joined.dtype)])
    order = jnp.arange(count)
    same = (block_owner[:, None] == block_owner[None, :]) & (order[None, :] < order[:, None])
    slot = block_owner * capacity + jnp.sum(same.astype(jnp.int32), axis=1)
    hits = slot[None, :] == jnp.arange(owners * capacity)[:, None]
    source = jnp.min(jnp.where(hits, order[None, :], count), axis=1)
    return joined[source]


def shards(
    x_edges,
    send_list,
    connectivity,
    elem_mats,
    elem_live,
    currents,
    positions,
    block_live,
    block_owner,
    block_leaf,
    cone_waves,
):
    owned, columns = x_edges.shape
    partitions, width = send_list.shape
    elements = connectivity.shape[1]
    everywhere = ("dom", "dir")

    list_row = send_list.reshape(1, partitions * width)
    outgoing = pick_rows(list_row, x_edges).reshape(partitions, width, columns)
    halo = lax.all_to_all(outgoing, everywhere, split_axis=0, concat_axis=0, tiled=True)

    list_lanes = jnp.broadcast_to(
        send_list.reshape(partitions * width, 1), (partitions * width, columns)
    )
    live = jnp.arange(elements)[None, :] < elem_live[0]
    mats = jnp.where(live, elem_mats, 0.0).T
    currents, list_lanes, mats = lax.optimization_barrier((currents, list_lanes, mats))
    packed = packed_blocks(currents, positions, block_live, block_owner, block_leaf)

    halo, packed, cone_waves = lax.optimization_barrier((halo, packed, cone_waves))
    arrived = lax.all_to_all(packed, "dom", split_axis=0, concat_axis=0, tiled=True)

    waves = [cone_waves]
    for s in range(1, DIRS):
        waves.append(lax.ppermute(cone_waves, "dir", [(i, (i - s) % DIRS) for i in range(DIRS)]))
    waves = jnp.concatenate(waves, axis=1) * (0.5 / math.pi)
    waves = jnp.broadcast_to(waves[:, :, None], waves.shape + (columns,))
    halo, waves = lax.optimization_barrier((halo, waves))
    local, back = element_sums(
        connectivity, x_edges, halo.reshape(partitions * width, columns), mats
    )
    back, arrived = lax.optimization_barrier((back, arrived))
    returned = lax.all_to_all(
        back.reshape(partitions, width, columns),
        everywhere,
        split_axis=0,
        concat_axis=0,
        tiled=True,
    )

    def onward(piece, s):
        return lax.ppermute(piece, "dir", [(i, (i + s) % DIRS) for i in range(DIRS)])

    half = jnp.bfloat16
    pieces = parent_sums(arrived, waves, (jnp.float32, half, half, half))
    moved = [onward(pieces[t], t) for t in range(1, DIRS)]
    interior_out = fold_back(list_lanes, returned.reshape(partitions * width, columns), local)
    interior_out, moved = lax.optimization_barrier((interior_out, moved))
    expansions = pieces[0]
    for piece in moved:
        expansions = expansions + piece.astype(jnp.float32)
    return (interior_out, expansions)


def solution(mesh):
    both = ("dom", "dir")
    placed = (
        P(both, None),
        P(both, None),
        P(None, both),
        P(None, both),
        P(both),
        P(both, None, None),
        P(both, None, None),
        P(both),
        P(both),
        P(both),
        P(None, "dir"),
    )
    return jax.shard_map(
        shards,
        mesh=mesh,
        in_specs=placed,
        out_specs=(P(both, None), P("dom", "dir", None, None, None)),
        check_vma=False,
    )
```

```python
import functools
import math

import jax
import jax.numpy as jnp
from jax import lax
from jax.experimental import pallas as pl
from jax.experimental.pallas import tpu as pltpu
from jax.sharding import PartitionSpec as P

NODES = 4
SQUARE = NODES**3
DIRS = 4
ROWS = 136
NODE_T = [math.cos((2 * j + 1) * math.pi / (2 * NODES)) for j in range(NODES)]


def vmem():
    return pl.BlockSpec(memory_space=pltpu.VMEM)


def smem():
    return pl.BlockSpec(memory_space=pltpu.SMEM)


def params(mebibytes):
    return pltpu.CompilerParams(vmem_limit_bytes=mebibytes * 1024 * 1024)


def pick_kernel(list_ref, x_ref, out_ref, flipped):
    owned, columns = x_ref.shape
    total = list_ref.shape[1]
    tile = min(1024, total)
    flipped[...] = x_ref[...].T

    def one(step, carry):
        at = pl.ds(pl.multiple_of(step * tile, tile), tile)
        rows = lax.broadcasted_iota(jnp.int32, (owned, tile), 0)
        hot = jnp.where(rows == list_ref[:, at], 1.0, 0.0).astype(flipped.dtype)
        picked = jnp.dot(flipped[...], hot, preferred_element_type=jnp.float32)
        out_ref[at, :] = picked.T.astype(out_ref.dtype)
        return carry

    lax.fori_loop(0, total // tile, one, 0)


def pick_rows(list_row, x_edges):
    owned, columns = x_edges.shape
    total = list_row.shape[1]
    return pl.pallas_call(
        pick_kernel,
        out_shape=jax.ShapeDtypeStruct((total, columns), x_edges.dtype),
        in_specs=[vmem(), vmem()],
        out_specs=vmem(),
        scratch_shapes=[pltpu.VMEM((columns, owned), x_edges.dtype)],
        compiler_params=params(24),
        cost_estimate=pl.CostEstimate(flops=0, bytes_accessed=1 << 24, transcendentals=0),
        name="pick_rows",
    )(list_row, x_edges)


GROUP = 8
PAIR = 2


def element_kernel(
    conn_ref, x_ref, halo_ref, mats_ref, local_ref, back_ref, table, stage, terms, *sums
):
    owned = x_ref.shape[0]
    halo = halo_ref.shape[0]
    elements = conn_ref.shape[1]
    columns = x_ref.shape[1]
    table[0:owned, :] = x_ref[...].astype(jnp.float32)
    table[owned : owned + halo, :] = halo_ref[...].astype(jnp.float32)
    for total in sums:
        total[...] = jnp.zeros_like(total)
    split = len(sums)

    def one(step, carry):
        for part in range(PAIR):
            first = (step * PAIR + part) * GROUP
            base = part * 6 * GROUP
            for j in range(6):
                for s in range(GROUP):
                    stage[base + j * GROUP + s : base + j * GROUP + s + 1, :] = table[
                        pl.ds(conn_ref[j, first + s], 1), :
                    ]
        for part in range(PAIR):
            first = (step * PAIR + part) * GROUP
            base = part * 6 * GROUP
            coefs = mats_ref[pl.ds(pl.multiple_of(first, GROUP), GROUP), :]
            values = [stage[base + j * GROUP : base + (j + 1) * GROUP, :] for j in range(6)]
            for i in range(6):
                term = None
                for j in range(6):
                    q = i * 6 + j
                    piece = jnp.broadcast_to(coefs[:, q : q + 1], (GROUP, columns)) * values[j]
                    term = piece if term is None else term + piece
                terms[base + i * GROUP : base + (i + 1) * GROUP, :] = term
        for part in range(PAIR):
            first = (step * PAIR + part) * GROUP
            base = part * 6 * GROUP
            for s in range(GROUP):
                for i in range(6):
                    row = pl.ds(conn_ref[i, first + s], 1)
                    at = base + i * GROUP + s
                    total = sums[i % split]
                    total[row, :] = total[row, :] + terms[at : at + 1, :]
        return carry

    lax.fori_loop(0, elements // (GROUP * PAIR), one, 0)

    def finish(step, carry):
        at = pl.ds(pl.multiple_of(step * 256, 256), 256)
        whole = sums[0][at, :]
        for total in sums[1:]:
            whole = whole + total[at, :]
        local_ref[at, :] = whole
        return carry

    lax.fori_loop(0, owned // 256, finish, 0)

    def finish_back(step, carry):
        at = pl.ds(pl.multiple_of(step * 256, 256), 256)
        src = pl.ds(pl.multiple_of(owned + step * 256, 256), 256)
        whole = sums[0][src, :]
        for total in sums[1:]:
            whole = whole + total[src, :]
        back_ref[at, :] = whole.astype(back_ref.dtype)
        return carry

    lax.fori_loop(0, halo // 256, finish_back, 0)


def element_sums(connectivity, x_edges, halo, mats):
    owned, columns = x_edges.shape
    slots = halo.shape[0]
    return pl.pallas_call(
        element_kernel,
        out_shape=(
            jax.ShapeDtypeStruct((owned, columns), jnp.float32),
            jax.ShapeDtypeStruct((slots, columns), jnp.bfloat16),
        ),
        in_specs=[smem(), vmem(), vmem(), vmem()],
        out_specs=(vmem(), vmem()),
        scratch_shapes=[
            pltpu.VMEM((owned + slots, columns), jnp.float32),
            pltpu.VMEM((6 * GROUP * PAIR, columns), jnp.float32),
            pltpu.VMEM((6 * GROUP * PAIR, columns), jnp.float32),
        ]
        + [pltpu.VMEM((owned + slots, columns), jnp.float32) for _ in range(6)],
        compiler_params=params(40),
        cost_estimate=pl.CostEstimate(flops=0, bytes_accessed=1 << 26, transcendentals=0),
        name="element_sums",
    )(connectivity, x_edges, halo, mats)


def fold_kernel(list_ref, returned_ref, local_ref, out_ref, flipped):
    owned, columns = local_ref.shape
    tile = FOLD_TILE
    flipped[...] = returned_ref[...].T
    lanes = lax.broadcasted_iota(jnp.int32, list_ref.shape, 1)

    def one(step, carry):
        hots = []
        for part in range(tile // columns):
            want = lanes + (step * tile + part * columns)
            hots.append(jnp.where(list_ref[...] == want, 1.0, 0.0).astype(flipped.dtype))
        total = jnp.dot(
            flipped[...], jnp.concatenate(hots, axis=1), preferred_element_type=jnp.float32
        )
        at = pl.ds(pl.multiple_of(step * tile, tile), tile)
        out_ref[at, :] = local_ref[at, :] + total.T
        return carry

    lax.fori_loop(0, owned // tile, one, 0)


FOLD_TILE = 512


def fold_back(list_lanes, returned, local):
    return pl.pallas_call(
        fold_kernel,
        out_shape=jax.ShapeDtypeStruct(local.shape, jnp.float32),
        in_specs=[vmem(), vmem(), vmem()],
        out_specs=vmem(),
        scratch_shapes=[pltpu.VMEM(returned.shape[::-1], returned.dtype)],
        compiler_params=params(50),
        cost_estimate=pl.CostEstimate(flops=1 << 32, bytes_accessed=1 << 24, transcendentals=0),
        name="fold_back",
    )(list_lanes, returned, local)


def sin_cos_turns(turns):
    reduced = turns - jnp.floor(turns + 0.5)
    half = reduced * math.pi
    square = half * half

    def series(coefs):
        total = jnp.full_like(square, coefs[-1])
        for coef in coefs[-2::-1]:
            total = total * square + coef
        return total

    sine = half * series([(-1) ** n / math.factorial(2 * n + 1) for n in range(6)])
    cosine = series([(-1) ** n / math.factorial(2 * n) for n in range(7)])
    return 2.0 * sine * cosine, 1.0 - 2.0 * sine * sine


def node_polynomials(coords):
    away = [coords - t for t in NODE_T]
    low, high = away[0] * away[1], away[2] * away[3]
    pairs = [away[1] * high, away[0] * high, low * away[3], low * away[2]]
    scaled = []
    for j in range(NODES):
        scale = math.prod(NODE_T[j] - NODE_T[i] for i in range(NODES) if i != j)
        scaled.append(pairs[j] * (1.0 / scale))
    return scaled


def parent_kernel(arrived_ref, waves_ref, *refs):
    outs, (blocks_ref, weights_0, sources_0, weights_1, sources_1, sums, landed) = (
        refs[:-7],
        refs[-7:],
    )
    slots, unused, columns = blocks_ref.shape
    cones = waves_ref.shape[1]
    size = columns
    per_dir = cones // len(outs)
    span = sources_0.shape[0] // size
    steps = slots // span

    def fetch(step):
        at = pl.ds(step * span, span)
        return pltpu.make_async_copy(arrived_ref.at[at], blocks_ref.at[at], landed.at[step])

    for step in range(steps):
        fetch(step).start()

    sub = lax.broadcasted_iota(jnp.int32, (8, size), 0)
    y_rows = lax.broadcasted_iota(jnp.int32, (size, columns), 0).astype(jnp.float32)
    y_rows = y_rows.astype(jnp.bfloat16)
    zero = jnp.zeros((size, columns), jnp.bfloat16)

    sums[...] = jnp.zeros_like(sums)

    def prepare(step, part, weights, sources):
        slot = step * span + part
        tail = blocks_ref[slot, size : size + 8, :]
        live = jnp.broadcast_to(tail[7:8, :], (size, columns))
        parent = jnp.broadcast_to(tail[6:7, :], (size, columns))
        block = jnp.where(y_rows < live, blocks_ref[slot, 0:size, :], zero)
        at = slice(part * size, (part + 1) * size)
        second_parent = parent > jnp.bfloat16(0.5)
        sources[at, 0:columns] = jnp.where(second_parent, zero, block)
        sources[at, columns : 2 * columns] = jnp.where(second_parent, block, zero)
        meta = tail.astype(jnp.float32)
        shifted = meta[0:3, :] + meta[3:6, :]
        turns = None
        for d in range(3):
            piece = waves_ref[d] * jnp.broadcast_to(shifted[d : d + 1, :], (cones, size))
            turns = piece if turns is None else turns + piece
        sine, cosine = sin_cos_turns(turns)
        along = node_polynomials(shifted * 0.5)

        def row(d, j):
            return jnp.broadcast_to(along[j][d : d + 1, :], (8, size))

        third = row(2, 3)
        for j in range(NODES - 1):
            third = jnp.where(sub % NODES == j, row(2, j), third)
        second = [
            jnp.where(sub < NODES, row(1, 2 * h), row(1, 2 * h + 1)) * third for h in range(2)
        ]
        first = [row(0, j) for j in range(NODES)]
        basis = jnp.concatenate([first[v // 2] * second[v % 2] for v in range(8)], axis=0)
        for k in range(cones):
            base = k * 2 * SQUARE
            weights[base : base + SQUARE, at] = (
                basis * jnp.broadcast_to(cosine[k : k + 1, :], (SQUARE, size))
            ).astype(jnp.bfloat16)
            weights[base + SQUARE : base + 2 * SQUARE, at] = (
                basis * jnp.broadcast_to(-sine[k : k + 1, :], (SQUARE, size))
            ).astype(jnp.bfloat16)

    height = min(512, cones * 2 * SQUARE)
    chunks = cones * 2 * SQUARE // height
    share = max(1, span // chunks)

    def work(weights, sources, step, later_weights, later_sources):
        for chunk in range(chunks):
            row = chunk * height
            sums[row : row + height, :] += jnp.dot(
                weights[row : row + height, :], sources[...], preferred_element_type=jnp.float32
            )
            for part in range(chunk * share, min(span, (chunk + 1) * share)):
                prepare(step, part, later_weights, later_sources)

    fetch(0).wait()
    for part in range(span):
        prepare(0, part, weights_0, sources_0)

    def two(pair, carry):
        later = jnp.minimum(2 * pair + 2, steps - 1)
        fetch(2 * pair + 1).wait()

        @pl.when(2 * pair + 2 < steps)
        def _():
            fetch(later).wait()

        work(weights_0, sources_0, 2 * pair + 1, weights_1, sources_1)
        work(weights_1, sources_1, later, weights_0, sources_0)
        return carry

    lax.fori_loop(0, steps // 2, two, 0)

    node_rows = lax.broadcasted_iota(jnp.int32, (SQUARE, columns), 0)

    def node_value(digit):
        value = jnp.full((SQUARE, columns), NODE_T[0], jnp.float32)
        for j in range(1, NODES):
            value = jnp.where(digit == j, NODE_T[j], value)
        return value

    nodes = [
        node_value(node_rows // (NODES * NODES)),
        node_value(node_rows // NODES % NODES),
        node_value(node_rows % NODES),
    ]
    for k in range(cones):
        turns = None
        for d in range(3):
            wave = jnp.broadcast_to(waves_ref[d, k : k + 1, :], (SQUARE, columns))
            piece = wave * nodes[d]
            turns = piece if turns is None else turns + piece
        sine, cosine = sin_cos_turns(2.0 * turns)
        base = k * 2 * SQUARE
        out = outs[k // per_dir]
        for p in range(2):
            cols = slice(p * columns, (p + 1) * columns)
            real = sums[base : base + SQUARE, cols]
            imag = sums[base + SQUARE : base + 2 * SQUARE, cols]
            out[p, k % per_dir, 0] = (cosine * real - sine * imag).astype(out.dtype)
            out[p, k % per_dir, 1] = (cosine * imag + sine * real).astype(out.dtype)


SPAN = 8


def parent_sums(blocks, waves, dtypes):
    columns = blocks.shape[2]
    cones = waves.shape[1]
    piece = (2, cones // len(dtypes), 2, SQUARE, columns)
    rows = cones * 2 * SQUARE
    return pl.pallas_call(
        parent_kernel,
        out_shape=tuple(jax.ShapeDtypeStruct(piece, dtype) for dtype in dtypes),
        in_specs=[pl.BlockSpec(memory_space=pl.ANY), vmem()],
        out_specs=(vmem(),) * len(dtypes),
        scratch_shapes=[
            pltpu.VMEM(blocks.shape, blocks.dtype),
            pltpu.VMEM((rows, SPAN * columns), jnp.bfloat16),
            pltpu.VMEM((SPAN * columns, 2 * columns), jnp.bfloat16),
            pltpu.VMEM((rows, SPAN * columns), jnp.bfloat16),
            pltpu.VMEM((SPAN * columns, 2 * columns), jnp.bfloat16),
            pltpu.VMEM((rows, 2 * columns), jnp.float32),
            pltpu.SemaphoreType.DMA((blocks.shape[0] // SPAN,)),
        ],
        compiler_params=params(60),
        cost_estimate=pl.CostEstimate(
            flops=2 * rows * 2 * columns * blocks.shape[0] * columns,
            bytes_accessed=1 << 23,
            transcendentals=0,
        ),
        name="parent_sums",
    )(blocks, waves)


def packed_blocks(currents, positions, block_live, block_owner, block_leaf):
    count, size, columns = currents.shape
    owners = lax.axis_size("dom")
    capacity = 3 * count // owners
    octant = block_leaf % 8
    digits = jnp.stack([octant // 4, octant // 2 % 2, octant % 2], axis=1)
    facts = jnp.concatenate(
        [2 * digits - 1, (block_leaf // 8)[:, None], block_live[:, None]], axis=1
    ).astype(jnp.bfloat16)
    joined = jnp.concatenate(
        [currents, positions, jnp.broadcast_to(facts[:, :, None], (count, 5, columns))], axis=1
    )
    joined = jnp.concatenate([joined, jnp.zeros((1, ROWS, columns), joined.dtype)])
    order = jnp.arange(count)
    same = (block_owner[:, None] == block_owner[None, :]) & (order[None, :] < order[:, None])
    slot = block_owner * capacity + jnp.sum(same.astype(jnp.int32), axis=1)
    hits = slot[None, :] == jnp.arange(owners * capacity)[:, None]
    source = jnp.min(jnp.where(hits, order[None, :], count), axis=1)
    return joined[source]


def shards(
    x_edges,
    send_list,
    connectivity,
    elem_mats,
    elem_live,
    currents,
    positions,
    block_live,
    block_owner,
    block_leaf,
    cone_waves,
):
    owned, columns = x_edges.shape
    partitions, width = send_list.shape
    elements = connectivity.shape[1]
    everywhere = ("dom", "dir")

    list_row = send_list.reshape(1, partitions * width)
    outgoing = pick_rows(list_row, x_edges).reshape(partitions, width, columns)
    halo = lax.all_to_all(outgoing, everywhere, split_axis=0, concat_axis=0, tiled=True)

    list_lanes = jnp.broadcast_to(
        send_list.reshape(partitions * width, 1), (partitions * width, columns)
    )
    live = jnp.arange(elements)[None, :] < elem_live[0]
    mats = jnp.where(live, elem_mats, 0.0).T
    currents, list_lanes, mats = lax.optimization_barrier((currents, list_lanes, mats))
    packed = packed_blocks(currents, positions, block_live, block_owner, block_leaf)

    halo, packed, cone_waves = lax.optimization_barrier((halo, packed, cone_waves))
    arrived = lax.all_to_all(packed, "dom", split_axis=0, concat_axis=0, tiled=True)

    waves = [cone_waves]
    for s in range(1, DIRS):
        waves.append(lax.ppermute(cone_waves, "dir", [(i, (i - s) % DIRS) for i in range(DIRS)]))
    waves = jnp.concatenate(waves, axis=1) * (0.5 / math.pi)
    waves = jnp.broadcast_to(waves[:, :, None], waves.shape + (columns,))
    halo, waves = lax.optimization_barrier((halo, waves))
    local, back = element_sums(
        connectivity, x_edges, halo.reshape(partitions * width, columns), mats
    )
    back, arrived = lax.optimization_barrier((back, arrived))
    returned = lax.all_to_all(
        back.reshape(partitions, width, columns),
        everywhere,
        split_axis=0,
        concat_axis=0,
        tiled=True,
    )

    def onward(piece, s):
        return lax.ppermute(piece, "dir", [(i, (i + s) % DIRS) for i in range(DIRS)])

    half = jnp.bfloat16
    pieces = parent_sums(arrived, waves, (jnp.float32, half, half, half))
    moved = [onward(pieces[t], t) for t in range(1, DIRS)]
    interior_out = fold_back(list_lanes, returned.reshape(partitions * width, columns), local)
    interior_out, moved = lax.optimization_barrier((interior_out, moved))
    expansions = pieces[0]
    for piece in moved:
        expansions = expansions + piece.astype(jnp.float32)
    return (interior_out, expansions)


def solution(mesh):
    both = ("dom", "dir")
    placed = (
        P(both, None),
        P(both, None),
        P(None, both),
        P(None, both),
        P(both),
        P(both, None, None),
        P(both, None, None),
        P(both),
        P(both),
        P(both),
        P(None, "dir"),
    )
    return jax.shard_map(
        shards,
        mesh=mesh,
        in_specs=placed,
        out_specs=(P(both, None), P("dom", "dir", None, None, None)),
        check_vma=False,
    )
```

```python
import functools
import math

import jax
import jax.numpy as jnp
from jax import lax
from jax.experimental import pallas as pl
from jax.experimental.pallas import tpu as pltpu
from jax.sharding import PartitionSpec as P

NODES = 4
SQUARE = NODES**3
DIRS = 4
ROWS = 136
NODE_T = [math.cos((2 * j + 1) * math.pi / (2 * NODES)) for j in range(NODES)]


def vmem():
    return pl.BlockSpec(memory_space=pltpu.VMEM)


def smem():
    return pl.BlockSpec(memory_space=pltpu.SMEM)


def params(mebibytes):
    return pltpu.CompilerParams(vmem_limit_bytes=mebibytes * 1024 * 1024)


def pick_kernel(list_ref, x_ref, out_ref, flipped):
    owned, columns = x_ref.shape
    total = list_ref.shape[1]
    tile = min(1024, total)
    flipped[...] = x_ref[...].T

    def one(step, carry):
        at = pl.ds(pl.multiple_of(step * tile, tile), tile)
        rows = lax.broadcasted_iota(jnp.int32, (owned, tile), 0)
        hot = jnp.where(rows == list_ref[:, at], 1.0, 0.0).astype(flipped.dtype)
        picked = jnp.dot(flipped[...], hot, preferred_element_type=jnp.float32)
        out_ref[at, :] = picked.T.astype(out_ref.dtype)
        return carry

    lax.fori_loop(0, total // tile, one, 0)


def pick_rows(list_row, x_edges):
    owned, columns = x_edges.shape
    total = list_row.shape[1]
    return pl.pallas_call(
        pick_kernel,
        out_shape=jax.ShapeDtypeStruct((total, columns), x_edges.dtype),
        in_specs=[vmem(), vmem()],
        out_specs=vmem(),
        scratch_shapes=[pltpu.VMEM((columns, owned), x_edges.dtype)],
        compiler_params=params(24),
        cost_estimate=pl.CostEstimate(flops=0, bytes_accessed=1 << 24, transcendentals=0),
        name="pick_rows",
    )(list_row, x_edges)


GROUP = 8
PAIR = 2


def element_kernel(
    conn_ref, x_ref, halo_ref, mats_ref, local_ref, back_ref, table, stage, terms, *sums
):
    owned = x_ref.shape[0]
    halo = halo_ref.shape[0]
    elements = conn_ref.shape[1]
    columns = x_ref.shape[1]
    table[0:owned, :] = x_ref[...].astype(jnp.float32)
    table[owned : owned + halo, :] = halo_ref[...].astype(jnp.float32)
    for total in sums:
        total[...] = jnp.zeros_like(total)
    split = len(sums)

    def one(step, carry):
        for part in range(PAIR):
            first = (step * PAIR + part) * GROUP
            base = part * 6 * GROUP
            for j in range(6):
                for s in range(GROUP):
                    stage[base + j * GROUP + s : base + j * GROUP + s + 1, :] = table[
                        pl.ds(conn_ref[j, first + s], 1), :
                    ]
        for part in range(PAIR):
            first = (step * PAIR + part) * GROUP
            base = part * 6 * GROUP
            coefs = mats_ref[pl.ds(pl.multiple_of(first, GROUP), GROUP), :]
            values = [stage[base + j * GROUP : base + (j + 1) * GROUP, :] for j in range(6)]
            for i in range(6):
                term = None
                for j in range(6):
                    q = i * 6 + j
                    piece = jnp.broadcast_to(coefs[:, q : q + 1], (GROUP, columns)) * values[j]
                    term = piece if term is None else term + piece
                terms[base + i * GROUP : base + (i + 1) * GROUP, :] = term
        for part in range(PAIR):
            first = (step * PAIR + part) * GROUP
            base = part * 6 * GROUP
            for s in range(GROUP):
                for i in range(6):
                    row = pl.ds(conn_ref[i, first + s], 1)
                    at = base + i * GROUP + s
                    total = sums[i % split]
                    total[row, :] = total[row, :] + terms[at : at + 1, :]
        return carry

    lax.fori_loop(0, elements // (GROUP * PAIR), one, 0)

    def finish(step, carry):
        at = pl.ds(pl.multiple_of(step * 256, 256), 256)
        whole = sums[0][at, :]
        for total in sums[1:]:
            whole = whole + total[at, :]
        local_ref[at, :] = whole
        return carry

    lax.fori_loop(0, owned // 256, finish, 0)

    def finish_back(step, carry):
        at = pl.ds(pl.multiple_of(step * 256, 256), 256)
        src = pl.ds(pl.multiple_of(owned + step * 256, 256), 256)
        whole = sums[0][src, :]
        for total in sums[1:]:
            whole = whole + total[src, :]
        back_ref[at, :] = whole.astype(back_ref.dtype)
        return carry

    lax.fori_loop(0, halo // 256, finish_back, 0)


def element_sums(connectivity, x_edges, halo, mats):
    owned, columns = x_edges.shape
    slots = halo.shape[0]
    return pl.pallas_call(
        element_kernel,
        out_shape=(
            jax.ShapeDtypeStruct((owned, columns), jnp.float32),
            jax.ShapeDtypeStruct((slots, columns), jnp.bfloat16),
        ),
        in_specs=[smem(), vmem(), vmem(), vmem()],
        out_specs=(vmem(), vmem()),
        scratch_shapes=[
            pltpu.VMEM((owned + slots, columns), jnp.float32),
            pltpu.VMEM((6 * GROUP * PAIR, columns), jnp.float32),
            pltpu.VMEM((6 * GROUP * PAIR, columns), jnp.float32),
        ]
        + [pltpu.VMEM((owned + slots, columns), jnp.float32) for _ in range(6)],
        compiler_params=params(40),
        cost_estimate=pl.CostEstimate(flops=0, bytes_accessed=1 << 26, transcendentals=0),
        name="element_sums",
    )(connectivity, x_edges, halo, mats)


def fold_kernel(list_ref, returned_ref, local_ref, out_ref, flipped):
    owned, columns = local_ref.shape
    tile = FOLD_TILE
    flipped[...] = returned_ref[...].T
    lanes = lax.broadcasted_iota(jnp.int32, list_ref.shape, 1)

    def one(step, carry):
        hots = []
        for part in range(tile // columns):
            want = lanes + (step * tile + part * columns)
            hots.append(jnp.where(list_ref[...] == want, 1.0, 0.0).astype(flipped.dtype))
        total = jnp.dot(
            flipped[...], jnp.concatenate(hots, axis=1), preferred_element_type=jnp.float32
        )
        at = pl.ds(pl.multiple_of(step * tile, tile), tile)
        out_ref[at, :] = local_ref[at, :] + total.T
        return carry

    lax.fori_loop(0, owned // tile, one, 0)


FOLD_TILE = 512


def fold_back(list_lanes, returned, local):
    return pl.pallas_call(
        fold_kernel,
        out_shape=jax.ShapeDtypeStruct(local.shape, jnp.float32),
        in_specs=[vmem(), vmem(), vmem()],
        out_specs=vmem(),
        scratch_shapes=[pltpu.VMEM(returned.shape[::-1], returned.dtype)],
        compiler_params=params(50),
        cost_estimate=pl.CostEstimate(flops=1 << 32, bytes_accessed=1 << 24, transcendentals=0),
        name="fold_back",
    )(list_lanes, returned, local)


def sin_cos_turns(turns):
    reduced = turns - jnp.floor(turns + 0.5)
    half = reduced * math.pi
    square = half * half

    def series(coefs):
        total = jnp.full_like(square, coefs[-1])
        for coef in coefs[-2::-1]:
            total = total * square + coef
        return total

    sine = half * series([(-1) ** n / math.factorial(2 * n + 1) for n in range(6)])
    cosine = series([(-1) ** n / math.factorial(2 * n) for n in range(7)])
    return 2.0 * sine * cosine, 1.0 - 2.0 * sine * sine


def node_polynomials(coords):
    away = [coords - t for t in NODE_T]
    low, high = away[0] * away[1], away[2] * away[3]
    pairs = [away[1] * high, away[0] * high, low * away[3], low * away[2]]
    scaled = []
    for j in range(NODES):
        scale = math.prod(NODE_T[j] - NODE_T[i] for i in range(NODES) if i != j)
        scaled.append(pairs[j] * (1.0 / scale))
    return scaled


def parent_kernel(arrived_ref, tables_ref, waves_ref, *refs):
    outs, scratch = refs[:-9], refs[-9:]
    blocks_ref, spin_ref, weights_0, sources_0, weights_1, sources_1, sums, landed, spun = scratch
    slots, unused, columns = blocks_ref.shape
    cones = waves_ref.shape[1]
    size = columns
    per_dir = cones // len(outs)
    span = sources_0.shape[0] // size
    steps = slots // span

    def fetch(step):
        at = pl.ds(step * span, span)
        return pltpu.make_async_copy(arrived_ref.at[at], blocks_ref.at[at], landed.at[step])

    for step in range(steps):
        fetch(step).start()
    turned = pltpu.make_async_copy(tables_ref, spin_ref, spun)
    turned.start()

    sub = lax.broadcasted_iota(jnp.int32, (8, size), 0)
    y_rows = lax.broadcasted_iota(jnp.int32, (size, columns), 0).astype(jnp.float32)
    y_rows = y_rows.astype(jnp.bfloat16)
    zero = jnp.zeros((size, columns), jnp.bfloat16)

    sums[...] = jnp.zeros_like(sums)

    def prepare(step, part, weights, sources):
        slot = step * span + part
        tail = blocks_ref[slot, size : size + 8, :]
        live = jnp.broadcast_to(tail[7:8, :], (size, columns))
        parent = jnp.broadcast_to(tail[6:7, :], (size, columns))
        block = jnp.where(y_rows < live, blocks_ref[slot, 0:size, :], zero)
        at = slice(part * size, (part + 1) * size)
        second_parent = parent > jnp.bfloat16(0.5)
        sources[at, 0:columns] = jnp.where(second_parent, zero, block)
        sources[at, columns : 2 * columns] = jnp.where(second_parent, block, zero)
        meta = tail.astype(jnp.float32)
        shifted = meta[0:3, :] + meta[3:6, :]
        turns = None
        for d in range(3):
            piece = waves_ref[d] * jnp.broadcast_to(shifted[d : d + 1, :], (cones, size))
            turns = piece if turns is None else turns + piece
        sine, cosine = sin_cos_turns(turns)
        along = node_polynomials(shifted * 0.5)

        def row(d, j):
            return jnp.broadcast_to(along[j][d : d + 1, :], (8, size))

        third = row(2, 3)
        for j in range(NODES - 1):
            third = jnp.where(sub % NODES == j, row(2, j), third)
        second = [
            jnp.where(sub < NODES, row(1, 2 * h), row(1, 2 * h + 1)) * third for h in range(2)
        ]
        first = [row(0, j) for j in range(NODES)]
        basis = jnp.concatenate([first[v // 2] * second[v % 2] for v in range(8)], axis=0)
        for k in range(cones):
            base = k * 2 * SQUARE
            weights[base : base + SQUARE, at] = (
                basis * jnp.broadcast_to(cosine[k : k + 1, :], (SQUARE, size))
            ).astype(jnp.bfloat16)
            weights[base + SQUARE : base + 2 * SQUARE, at] = (
                basis * jnp.broadcast_to(-sine[k : k + 1, :], (SQUARE, size))
            ).astype(jnp.bfloat16)

    height = min(512, cones * 2 * SQUARE)
    chunks = cones * 2 * SQUARE // height
    share = max(1, span // chunks)

    def work(weights, sources, step, later_weights, later_sources):
        for chunk in range(chunks):
            row = chunk * height
            sums[row : row + height, :] += jnp.dot(
                weights[row : row + height, :], sources[...], preferred_element_type=jnp.float32
            )
            for part in range(chunk * share, min(span, (chunk + 1) * share)):
                prepare(step, part, later_weights, later_sources)

    fetch(0).wait()
    for part in range(span):
        prepare(0, part, weights_0, sources_0)

    def two(pair, carry):
        later = jnp.minimum(2 * pair + 2, steps - 1)
        fetch(2 * pair + 1).wait()

        @pl.when(2 * pair + 2 < steps)
        def _():
            fetch(later).wait()

        work(weights_0, sources_0, 2 * pair + 1, weights_1, sources_1)
        work(weights_1, sources_1, later, weights_0, sources_0)
        return carry

    lax.fori_loop(0, steps // 2, two, 0)

    turned.wait()
    for k in range(cones):
        cosine, sine = spin_ref[k, 0], spin_ref[k, 1]
        base = k * 2 * SQUARE
        out = outs[k // per_dir]
        for p in range(2):
            cols = slice(p * columns, (p + 1) * columns)
            real = sums[base : base + SQUARE, cols]
            imag = sums[base + SQUARE : base + 2 * SQUARE, cols]
            out[p, k % per_dir, 0] = (cosine * real - sine * imag).astype(out.dtype)
            out[p, k % per_dir, 1] = (cosine * imag + sine * real).astype(out.dtype)


SPAN = 8


def parent_sums(blocks, tables, waves, dtypes):
    columns = blocks.shape[2]
    cones = waves.shape[1]
    piece = (2, cones // len(dtypes), 2, SQUARE, columns)
    rows = cones * 2 * SQUARE
    return pl.pallas_call(
        parent_kernel,
        out_shape=tuple(jax.ShapeDtypeStruct(piece, dtype) for dtype in dtypes),
        in_specs=[pl.BlockSpec(memory_space=pl.ANY)] * 2 + [vmem()],
        out_specs=(vmem(),) * len(dtypes),
        scratch_shapes=[
            pltpu.VMEM(blocks.shape, blocks.dtype),
            pltpu.VMEM(tables.shape, tables.dtype),
            pltpu.VMEM((rows, SPAN * columns), jnp.bfloat16),
            pltpu.VMEM((SPAN * columns, 2 * columns), jnp.bfloat16),
            pltpu.VMEM((rows, SPAN * columns), jnp.bfloat16),
            pltpu.VMEM((SPAN * columns, 2 * columns), jnp.bfloat16),
            pltpu.VMEM((rows, 2 * columns), jnp.float32),
            pltpu.SemaphoreType.DMA((blocks.shape[0] // SPAN,)),
            pltpu.SemaphoreType.DMA,
        ],
        compiler_params=params(60),
        cost_estimate=pl.CostEstimate(
            flops=2 * rows * 2 * columns * blocks.shape[0] * columns,
            bytes_accessed=1 << 23,
            transcendentals=0,
        ),
        name="parent_sums",
    )(blocks, tables, waves)


def packed_blocks(currents, positions, block_live, block_owner, block_leaf):
    count, size, columns = currents.shape
    owners = lax.axis_size("dom")
    capacity = 3 * count // owners
    octant = block_leaf % 8
    digits = jnp.stack([octant // 4, octant // 2 % 2, octant % 2], axis=1)
    facts = jnp.concatenate(
        [2 * digits - 1, (block_leaf // 8)[:, None], block_live[:, None]], axis=1
    ).astype(jnp.bfloat16)
    joined = jnp.concatenate(
        [currents, positions, jnp.broadcast_to(facts[:, :, None], (count, 5, columns))], axis=1
    )
    joined = jnp.concatenate([joined, jnp.zeros((1, ROWS, columns), joined.dtype)])
    order = jnp.arange(count)
    same = (block_owner[:, None] == block_owner[None, :]) & (order[None, :] < order[:, None])
    slot = block_owner * capacity + jnp.sum(same.astype(jnp.int32), axis=1)
    hits = slot[None, :] == jnp.arange(owners * capacity)[:, None]
    source = jnp.min(jnp.where(hits, order[None, :], count), axis=1)
    return joined[source]


def shards(
    x_edges,
    send_list,
    connectivity,
    elem_mats,
    elem_live,
    currents,
    positions,
    block_live,
    block_owner,
    block_leaf,
    cone_waves,
):
    owned, columns = x_edges.shape
    partitions, width = send_list.shape
    elements = connectivity.shape[1]
    everywhere = ("dom", "dir")

    list_row = send_list.reshape(1, partitions * width)
    outgoing = pick_rows(list_row, x_edges).reshape(partitions, width, columns)
    halo = lax.all_to_all(outgoing, everywhere, split_axis=0, concat_axis=0, tiled=True)

    list_lanes = jnp.broadcast_to(
        send_list.reshape(partitions * width, 1), (partitions * width, columns)
    )
    live = jnp.arange(elements)[None, :] < elem_live[0]
    mats = jnp.where(live, elem_mats, 0.0).T
    currents, list_lanes, mats = lax.optimization_barrier((currents, list_lanes, mats))
    packed = packed_blocks(currents, positions, block_live, block_owner, block_leaf)

    halo, packed, cone_waves = lax.optimization_barrier((halo, packed, cone_waves))
    arrived = lax.all_to_all(packed, "dom", split_axis=0, concat_axis=0, tiled=True)

    waves = [cone_waves]
    for s in range(1, DIRS):
        waves.append(lax.ppermute(cone_waves, "dir", [(i, (i - s) % DIRS) for i in range(DIRS)]))
    waves = jnp.concatenate(waves, axis=1) * (0.5 / math.pi)
    digits = jnp.arange(SQUARE)[None, :] // jnp.array([[NODES * NODES], [NODES], [1]]) % NODES
    nodes = jnp.cos((2.0 * digits + 1.0) * (math.pi / (2.0 * NODES)))
    turns = sum(waves[d][:, None] * nodes[d][None, :] for d in range(3))
    sine, cosine = sin_cos_turns(2.0 * turns)
    tables = jnp.stack([cosine, sine], axis=1)[..., None]
    tables = jnp.broadcast_to(tables, tables.shape[:-1] + (columns,))
    waves = jnp.broadcast_to(waves[:, :, None], waves.shape + (columns,))
    halo, waves, tables = lax.optimization_barrier((halo, waves, tables))
    local, back = element_sums(
        connectivity, x_edges, halo.reshape(partitions * width, columns), mats
    )
    back, arrived = lax.optimization_barrier((back, arrived))
    returned = lax.all_to_all(
        back.reshape(partitions, width, columns),
        everywhere,
        split_axis=0,
        concat_axis=0,
        tiled=True,
    )

    def onward(piece, s):
        return lax.ppermute(piece, "dir", [(i, (i + s) % DIRS) for i in range(DIRS)])

    half = jnp.bfloat16
    pieces = parent_sums(arrived, tables, waves, (jnp.float32, half, half, half))
    moved = [onward(pieces[t], t) for t in range(1, DIRS)]
    interior_out = fold_back(list_lanes, returned.reshape(partitions * width, columns), local)
    interior_out, moved = lax.optimization_barrier((interior_out, moved))
    expansions = pieces[0]
    for piece in moved:
        expansions = expansions + piece.astype(jnp.float32)
    return (interior_out, expansions)


def solution(mesh):
    both = ("dom", "dir")
    placed = (
        P(both, None),
        P(both, None),
        P(None, both),
        P(None, both),
        P(both),
        P(both, None, None),
        P(both, None, None),
        P(both),
        P(both),
        P(both),
        P(None, "dir"),
    )
    return jax.shard_map(
        shards,
        mesh=mesh,
        in_specs=placed,
        out_specs=(P(both, None), P("dom", "dir", None, None, None)),
        check_vma=False,
    )
```

```python
import functools
import math

import jax
import jax.numpy as jnp
from jax import lax
from jax.experimental import pallas as pl
from jax.experimental.pallas import tpu as pltpu
from jax.sharding import PartitionSpec as P

NODES = 4
SQUARE = NODES**3
DIRS = 4
ROWS = 136
NODE_T = [math.cos((2 * j + 1) * math.pi / (2 * NODES)) for j in range(NODES)]


def vmem():
    return pl.BlockSpec(memory_space=pltpu.VMEM)


def smem():
    return pl.BlockSpec(memory_space=pltpu.SMEM)


def params(mebibytes):
    return pltpu.CompilerParams(vmem_limit_bytes=mebibytes * 1024 * 1024)


def pick_kernel(list_ref, x_ref, out_ref, flipped):
    owned, columns = x_ref.shape
    total = list_ref.shape[1]
    tile = min(1024, total)
    flipped[...] = x_ref[...].T

    def one(step, carry):
        at = pl.ds(pl.multiple_of(step * tile, tile), tile)
        rows = lax.broadcasted_iota(jnp.int32, (owned, tile), 0)
        hot = jnp.where(rows == list_ref[:, at], 1.0, 0.0).astype(flipped.dtype)
        picked = jnp.dot(flipped[...], hot, preferred_element_type=jnp.float32)
        out_ref[at, :] = picked.T.astype(out_ref.dtype)
        return carry

    lax.fori_loop(0, total // tile, one, 0)


def pick_rows(list_row, x_edges):
    owned, columns = x_edges.shape
    total = list_row.shape[1]
    return pl.pallas_call(
        pick_kernel,
        out_shape=jax.ShapeDtypeStruct((total, columns), x_edges.dtype),
        in_specs=[vmem(), vmem()],
        out_specs=vmem(),
        scratch_shapes=[pltpu.VMEM((columns, owned), x_edges.dtype)],
        compiler_params=params(24),
        cost_estimate=pl.CostEstimate(flops=0, bytes_accessed=1 << 24, transcendentals=0),
        name="pick_rows",
    )(list_row, x_edges)


GROUP = 8
PAIR = 2


def element_kernel(
    conn_ref, x_ref, halo_ref, mats_ref, local_ref, back_ref, table, stage, terms, *sums
):
    owned = x_ref.shape[0]
    halo = halo_ref.shape[0]
    elements = conn_ref.shape[1]
    columns = x_ref.shape[1]
    table[0:owned, :] = x_ref[...].astype(jnp.float32)
    table[owned : owned + halo, :] = halo_ref[...].astype(jnp.float32)
    for total in sums:
        total[...] = jnp.zeros_like(total)
    split = len(sums)

    def one(step, carry):
        for part in range(PAIR):
            first = (step * PAIR + part) * GROUP
            base = part * 6 * GROUP
            for j in range(6):
                for s in range(GROUP):
                    stage[base + j * GROUP + s : base + j * GROUP + s + 1, :] = table[
                        pl.ds(conn_ref[j, first + s], 1), :
                    ]
        for part in range(PAIR):
            first = (step * PAIR + part) * GROUP
            base = part * 6 * GROUP
            coefs = mats_ref[pl.ds(pl.multiple_of(first, GROUP), GROUP), :]
            values = [stage[base + j * GROUP : base + (j + 1) * GROUP, :] for j in range(6)]
            for i in range(6):
                term = None
                for j in range(6):
                    q = i * 6 + j
                    piece = jnp.broadcast_to(coefs[:, q : q + 1], (GROUP, columns)) * values[j]
                    term = piece if term is None else term + piece
                terms[base + i * GROUP : base + (i + 1) * GROUP, :] = term
        for part in range(PAIR):
            first = (step * PAIR + part) * GROUP
            base = part * 6 * GROUP
            for s in range(GROUP):
                for i in range(6):
                    row = pl.ds(conn_ref[i, first + s], 1)
                    at = base + i * GROUP + s
                    total = sums[i % split]
                    total[row, :] = total[row, :] + terms[at : at + 1, :]
        return carry

    lax.fori_loop(0, elements // (GROUP * PAIR), one, 0)

    def finish(step, carry):
        at = pl.ds(pl.multiple_of(step * 256, 256), 256)
        whole = sums[0][at, :]
        for total in sums[1:]:
            whole = whole + total[at, :]
        local_ref[at, :] = whole
        return carry

    lax.fori_loop(0, owned // 256, finish, 0)

    def finish_back(step, carry):
        at = pl.ds(pl.multiple_of(step * 256, 256), 256)
        src = pl.ds(pl.multiple_of(owned + step * 256, 256), 256)
        whole = sums[0][src, :]
        for total in sums[1:]:
            whole = whole + total[src, :]
        back_ref[at, :] = whole.astype(back_ref.dtype)
        return carry

    lax.fori_loop(0, halo // 256, finish_back, 0)


def element_sums(connectivity, x_edges, halo, mats):
    owned, columns = x_edges.shape
    slots = halo.shape[0]
    return pl.pallas_call(
        element_kernel,
        out_shape=(
            jax.ShapeDtypeStruct((owned, columns), jnp.float32),
            jax.ShapeDtypeStruct((slots, columns), jnp.bfloat16),
        ),
        in_specs=[smem(), vmem(), vmem(), vmem()],
        out_specs=(vmem(), vmem()),
        scratch_shapes=[
            pltpu.VMEM((owned + slots, columns), jnp.float32),
            pltpu.VMEM((6 * GROUP * PAIR, columns), jnp.float32),
            pltpu.VMEM((6 * GROUP * PAIR, columns), jnp.float32),
        ]
        + [pltpu.VMEM((owned + slots, columns), jnp.float32) for _ in range(6)],
        compiler_params=params(40),
        cost_estimate=pl.CostEstimate(flops=0, bytes_accessed=1 << 26, transcendentals=0),
        name="element_sums",
    )(connectivity, x_edges, halo, mats)


def fold_kernel(list_ref, returned_ref, local_ref, out_ref, flipped):
    owned, columns = local_ref.shape
    tile = FOLD_TILE
    flipped[...] = returned_ref[...].T
    lanes = lax.broadcasted_iota(jnp.int32, list_ref.shape, 1)

    def one(step, carry):
        hots = []
        for part in range(tile // columns):
            want = lanes + (step * tile + part * columns)
            hots.append(jnp.where(list_ref[...] == want, 1.0, 0.0).astype(flipped.dtype))
        total = jnp.dot(
            flipped[...], jnp.concatenate(hots, axis=1), preferred_element_type=jnp.float32
        )
        at = pl.ds(pl.multiple_of(step * tile, tile), tile)
        out_ref[at, :] = local_ref[at, :] + total.T
        return carry

    lax.fori_loop(0, owned // tile, one, 0)


FOLD_TILE = 512


def fold_back(list_lanes, returned, local):
    return pl.pallas_call(
        fold_kernel,
        out_shape=jax.ShapeDtypeStruct(local.shape, jnp.float32),
        in_specs=[vmem(), vmem(), vmem()],
        out_specs=vmem(),
        scratch_shapes=[pltpu.VMEM(returned.shape[::-1], returned.dtype)],
        compiler_params=params(50),
        cost_estimate=pl.CostEstimate(flops=1 << 32, bytes_accessed=1 << 24, transcendentals=0),
        name="fold_back",
    )(list_lanes, returned, local)


def sin_cos_turns(turns):
    reduced = turns - jnp.floor(turns + 0.5)
    half = reduced * math.pi
    square = half * half

    def series(coefs):
        total = jnp.full_like(square, coefs[-1])
        for coef in coefs[-2::-1]:
            total = total * square + coef
        return total

    sine = half * series([(-1) ** n / math.factorial(2 * n + 1) for n in range(6)])
    cosine = series([(-1) ** n / math.factorial(2 * n) for n in range(7)])
    return 2.0 * sine * cosine, 1.0 - 2.0 * sine * sine


def node_polynomials(coords):
    away = [coords - t for t in NODE_T]
    low, high = away[0] * away[1], away[2] * away[3]
    pairs = [away[1] * high, away[0] * high, low * away[3], low * away[2]]
    scaled = []
    for j in range(NODES):
        scale = math.prod(NODE_T[j] - NODE_T[i] for i in range(NODES) if i != j)
        scaled.append(pairs[j] * (1.0 / scale))
    return scaled


def parent_kernel(arrived_ref, tables_ref, waves_ref, *refs):
    outs, scratch = refs[:-9], refs[-9:]
    blocks_ref, spin_ref, weights_0, sources_0, weights_1, sources_1, sums, landed, spun = scratch
    slots, unused, columns = blocks_ref.shape
    cones = waves_ref.shape[1]
    size = columns
    per_dir = cones // len(outs)
    span = sources_0.shape[0] // size
    steps = slots // span

    def fetch(step):
        at = pl.ds(step * span, span)
        return pltpu.make_async_copy(arrived_ref.at[at], blocks_ref.at[at], landed.at[step])

    for step in range(steps):
        fetch(step).start()
    turned = pltpu.make_async_copy(tables_ref, spin_ref, spun)
    turned.start()

    sub = lax.broadcasted_iota(jnp.int32, (8, size), 0)
    y_rows = lax.broadcasted_iota(jnp.int32, (size, columns), 0).astype(jnp.float32)
    y_rows = y_rows.astype(jnp.bfloat16)
    zero = jnp.zeros((size, columns), jnp.bfloat16)

    sums[...] = jnp.zeros_like(sums)

    def prepare(step, part, weights, sources):
        slot = step * span + part
        tail = blocks_ref[slot, size : size + 8, :]
        live = jnp.broadcast_to(tail[7:8, :], (size, columns))
        parent = jnp.broadcast_to(tail[6:7, :], (size, columns))
        block = jnp.where(y_rows < live, blocks_ref[slot, 0:size, :], zero)
        at = slice(part * size, (part + 1) * size)
        second_parent = parent > jnp.bfloat16(0.5)
        sources[at, 0:columns] = jnp.where(second_parent, zero, block)
        sources[at, columns : 2 * columns] = jnp.where(second_parent, block, zero)
        meta = tail.astype(jnp.float32)
        shifted = meta[0:3, :] + meta[3:6, :]
        turns = None
        for d in range(3):
            piece = waves_ref[d] * jnp.broadcast_to(shifted[d : d + 1, :], (cones, size))
            turns = piece if turns is None else turns + piece
        sine, cosine = sin_cos_turns(turns)
        along = node_polynomials(shifted * 0.5)

        def row(d, j):
            return jnp.broadcast_to(along[j][d : d + 1, :], (8, size))

        third = row(2, 3)
        for j in range(NODES - 1):
            third = jnp.where(sub % NODES == j, row(2, j), third)
        second = [
            jnp.where(sub < NODES, row(1, 2 * h), row(1, 2 * h + 1)) * third for h in range(2)
        ]
        first = [row(0, j) for j in range(NODES)]
        basis = jnp.concatenate([first[v // 2] * second[v % 2] for v in range(8)], axis=0)
        for k in range(cones):
            base = k * 2 * SQUARE
            weights[base : base + SQUARE, at] = (
                basis * jnp.broadcast_to(cosine[k : k + 1, :], (SQUARE, size))
            ).astype(jnp.bfloat16)
            weights[base + SQUARE : base + 2 * SQUARE, at] = (
                basis * jnp.broadcast_to(-sine[k : k + 1, :], (SQUARE, size))
            ).astype(jnp.bfloat16)

    height = min(1024, cones * 2 * SQUARE)
    chunks = cones * 2 * SQUARE // height
    share = max(1, span // chunks)

    def work(weights, sources, step, later_weights, later_sources):
        for chunk in range(chunks):
            row = chunk * height
            sums[row : row + height, :] += jnp.dot(
                weights[row : row + height, :], sources[...], preferred_element_type=jnp.float32
            )
            for part in range(chunk * share, min(span, (chunk + 1) * share)):
                prepare(step, part, later_weights, later_sources)

    fetch(0).wait()
    for part in range(span):
        prepare(0, part, weights_0, sources_0)

    def two(pair, carry):
        later = jnp.minimum(2 * pair + 2, steps - 1)
        fetch(2 * pair + 1).wait()

        @pl.when(2 * pair + 2 < steps)
        def _():
            fetch(later).wait()

        work(weights_0, sources_0, 2 * pair + 1, weights_1, sources_1)
        work(weights_1, sources_1, later, weights_0, sources_0)
        return carry

    lax.fori_loop(0, steps // 2, two, 0)

    turned.wait()
    for k in range(cones):
        cosine, sine = spin_ref[k, 0], spin_ref[k, 1]
        base = k * 2 * SQUARE
        out = outs[k // per_dir]
        for p in range(2):
            cols = slice(p * columns, (p + 1) * columns)
            real = sums[base : base + SQUARE, cols]
            imag = sums[base + SQUARE : base + 2 * SQUARE, cols]
            out[p, k % per_dir, 0] = (cosine * real - sine * imag).astype(out.dtype)
            out[p, k % per_dir, 1] = (cosine * imag + sine * real).astype(out.dtype)


SPAN = 8


def parent_sums(blocks, tables, waves, dtypes):
    columns = blocks.shape[2]
    cones = waves.shape[1]
    piece = (2, cones // len(dtypes), 2, SQUARE, columns)
    rows = cones * 2 * SQUARE
    return pl.pallas_call(
        parent_kernel,
        out_shape=tuple(jax.ShapeDtypeStruct(piece, dtype) for dtype in dtypes),
        in_specs=[pl.BlockSpec(memory_space=pl.ANY)] * 2 + [vmem()],
        out_specs=(vmem(),) * len(dtypes),
        scratch_shapes=[
            pltpu.VMEM(blocks.shape, blocks.dtype),
            pltpu.VMEM(tables.shape, tables.dtype),
            pltpu.VMEM((rows, SPAN * columns), jnp.bfloat16),
            pltpu.VMEM((SPAN * columns, 2 * columns), jnp.bfloat16),
            pltpu.VMEM((rows, SPAN * columns), jnp.bfloat16),
            pltpu.VMEM((SPAN * columns, 2 * columns), jnp.bfloat16),
            pltpu.VMEM((rows, 2 * columns), jnp.float32),
            pltpu.SemaphoreType.DMA((blocks.shape[0] // SPAN,)),
            pltpu.SemaphoreType.DMA,
        ],
        compiler_params=params(60),
        cost_estimate=pl.CostEstimate(
            flops=2 * rows * 2 * columns * blocks.shape[0] * columns,
            bytes_accessed=1 << 23,
            transcendentals=0,
        ),
        name="parent_sums",
    )(blocks, tables, waves)


def packed_blocks(currents, positions, block_live, block_owner, block_leaf):
    count, size, columns = currents.shape
    owners = lax.axis_size("dom")
    capacity = 3 * count // owners
    octant = block_leaf % 8
    digits = jnp.stack([octant // 4, octant // 2 % 2, octant % 2], axis=1)
    facts = jnp.concatenate(
        [2 * digits - 1, (block_leaf // 8)[:, None], block_live[:, None]], axis=1
    ).astype(jnp.bfloat16)
    joined = jnp.concatenate(
        [currents, positions, jnp.broadcast_to(facts[:, :, None], (count, 5, columns))], axis=1
    )
    joined = jnp.concatenate([joined, jnp.zeros((1, ROWS, columns), joined.dtype)])
    order = jnp.arange(count)
    same = (block_owner[:, None] == block_owner[None, :]) & (order[None, :] < order[:, None])
    slot = block_owner * capacity + jnp.sum(same.astype(jnp.int32), axis=1)
    hits = slot[None, :] == jnp.arange(owners * capacity)[:, None]
    source = jnp.min(jnp.where(hits, order[None, :], count), axis=1)
    return joined[source]


def shards(
    x_edges,
    send_list,
    connectivity,
    elem_mats,
    elem_live,
    currents,
    positions,
    block_live,
    block_owner,
    block_leaf,
    cone_waves,
):
    owned, columns = x_edges.shape
    partitions, width = send_list.shape
    elements = connectivity.shape[1]
    everywhere = ("dom", "dir")

    list_row = send_list.reshape(1, partitions * width)
    outgoing = pick_rows(list_row, x_edges).reshape(partitions, width, columns)
    halo = lax.all_to_all(outgoing, everywhere, split_axis=0, concat_axis=0, tiled=True)

    list_lanes = jnp.broadcast_to(
        send_list.reshape(partitions * width, 1), (partitions * width, columns)
    )
    live = jnp.arange(elements)[None, :] < elem_live[0]
    mats = jnp.where(live, elem_mats, 0.0).T
    currents, list_lanes, mats = lax.optimization_barrier((currents, list_lanes, mats))
    packed = packed_blocks(currents, positions, block_live, block_owner, block_leaf)

    halo, packed, cone_waves = lax.optimization_barrier((halo, packed, cone_waves))
    arrived = lax.all_to_all(packed, "dom", split_axis=0, concat_axis=0, tiled=True)

    waves = [cone_waves]
    for s in range(1, DIRS):
        waves.append(lax.ppermute(cone_waves, "dir", [(i, (i - s) % DIRS) for i in range(DIRS)]))
    waves = jnp.concatenate(waves, axis=1) * (0.5 / math.pi)
    digits = jnp.arange(SQUARE)[None, :] // jnp.array([[NODES * NODES], [NODES], [1]]) % NODES
    nodes = jnp.cos((2.0 * digits + 1.0) * (math.pi / (2.0 * NODES)))
    turns = sum(waves[d][:, None] * nodes[d][None, :] for d in range(3))
    sine, cosine = sin_cos_turns(2.0 * turns)
    tables = jnp.stack([cosine, sine], axis=1)[..., None]
    tables = jnp.broadcast_to(tables, tables.shape[:-1] + (columns,))
    waves = jnp.broadcast_to(waves[:, :, None], waves.shape + (columns,))
    halo, waves, tables = lax.optimization_barrier((halo, waves, tables))
    local, back = element_sums(
        connectivity, x_edges, halo.reshape(partitions * width, columns), mats
    )
    back, arrived = lax.optimization_barrier((back, arrived))
    returned = lax.all_to_all(
        back.reshape(partitions, width, columns),
        everywhere,
        split_axis=0,
        concat_axis=0,
        tiled=True,
    )

    def onward(piece, s):
        return lax.ppermute(piece, "dir", [(i, (i + s) % DIRS) for i in range(DIRS)])

    half = jnp.bfloat16
    pieces = parent_sums(arrived, tables, waves, (jnp.float32, half, half, half))
    moved = [onward(pieces[t], t) for t in (2, 1, 3)]
    interior_out = fold_back(list_lanes, returned.reshape(partitions * width, columns), local)
    interior_out, moved = lax.optimization_barrier((interior_out, moved))
    expansions = pieces[0]
    for piece in moved:
        expansions = expansions + piece.astype(jnp.float32)
    return (interior_out, expansions)


def solution(mesh):
    both = ("dom", "dir")
    placed = (
        P(both, None),
        P(both, None),
        P(None, both),
        P(None, both),
        P(both),
        P(both, None, None),
        P(both, None, None),
        P(both),
        P(both),
        P(both),
        P(None, "dir"),
    )
    return jax.shard_map(
        shards,
        mesh=mesh,
        in_specs=placed,
        out_specs=(P(both, None), P("dom", "dir", None, None, None)),
        check_vma=False,
    )
```
